128 devices in a mesh: dp: 16 (over z, x), section: 8 (over y, core).
Axes of the slice: x: 4, y: 4, z: 4, core: 2. Of those that a mesh axis runs over, the one named last changes fastest.
Arguments:
- saved_inputs: bfloat16 [8, 12288, 1024], P('section', 'dp'), may hold values from -6 to 6
- cotangent: bfloat16 [12288, 1024], P('dp'), may hold values from -6 to 6
- pack_lists: int32 [16, 768], P('dp'), may hold values from 0 to 767, each once within a row
- segment_ids: int32 [192, 64], P('dp'), may hold values from 0 to 7, never falling along the last dimension, each value on 1 to 32 neighbouring positions
- w_in: bfloat16 [8, 1024, 4096], P('section'), may hold values from -0.1875 to 0.1875
- w_out: bfloat16 [8, 1024, 1024], P('section'), may hold values from -0.1875 to 0.1875
Outputs:
- grad_inputs: bfloat16 [8, 12288, 1024], P('section', 'dp')
- grad_w_in: float32 [8, 1024, 4096], P('section', 'dp')
- grad_w_out: float32 [8, 1024, 1024], P('section', 'dp')
The draws below stay inside these ranges and needn't reach their ends.
Inputs may be any that keep to these rules, and one draw needn't show every extreme that they name: `pack_lists`: each row is an ordering of the rows of one loader rank; its k-th block of equal length names the rows sent to packed rank k. `segment_ids`: ids never fall along a micro-batch; a history is the run of one id, 1 to 32 rows, and one has exactly 32.
All inputs are finite; a program needn't handle non-finite values.
Results may differ from the reference program's by a relative error of at most 0.03.
Values may be sent and summed in bfloat16 or wider, within the bound.
No kernel may reach another device: no remote copies, remote signals or barrier semaphores. Data moves between devices by JAX's collectives and lax.ppermute only.
A program may use at most 128 MiB of HBM per device.

```python
import math
import jax
import jax.numpy as jnp
import numpy as np
from jax import lax

D = 1024
H = 16
MB_ROWS = 64
SEQ_MAX = 8
TOK_DEV = 768
TOKENS = 12288
LAYERS = 8
N_DP = 16
N_SECTION = 8


def raised(entries, rng, source, target, blocks, factor):
    def block_of(dim):
        return (jnp.arange(entries.shape[dim]) // (entries.shape[dim] // blocks)).reshape((-1,) + (1,) * (entries.ndim - 1 - dim))

    one_side = jax.random.permutation(rng, blocks)[block_of(target)]
    second = (block_of(target) + blocks // 2) % blocks
    return jnp.where((block_of(source) == one_side) | (block_of(source) == second), factor * entries, entries)


def levels(rng, dims, shards, smallest, high):
    factor_of = 1.0
    for axis_at, parts in shards:
        steps = jax.random.uniform(jax.random.fold_in(jax.random.fold_in(rng, 6), axis_at), (parts,), jnp.float32, smallest / len(shards), high / len(shards))
        factor_of = factor_of * jnp.repeat(jnp.exp(steps), dims[axis_at] // parts).reshape((-1,) + (1,) * (len(dims) - 1 - axis_at))
    return factor_of


def split_up(number_of, total, most, skew):
    weights = [(1 << 20) // math.isqrt(grade ** skew) + 1 for grade in range(2, number_of + 1)]
    spare, holding = total - most - (number_of - 1), [1] * (number_of - 1)
    while spare > 0:
        free = [i for i in range(number_of - 1) if holding[i] < most]
        pool, left = sum([weights[i] for i in free]), spare
        for i in free:
            extra = min(most - holding[i], max(1, left * weights[i] // pool), spare)
            holding[i] = holding[i] + extra
            spare = spare - extra
    return np.array([most] + holding)


def uneven_parts(stream_key, amount, total, bound, skew):
    if amount == 2:
        one = jax.random.randint(stream_key, (), max(1, total - bound), min(bound, total - 1) + 1)
        return jnp.stack([one, total - one])
    lengths = jnp.asarray(split_up(amount, total, bound, skew), jnp.int32)
    couples = (amount - 1) // 2
    donor, receiver = lengths[1:1 + 2 * couples:2], lengths[2:2 + 2 * couples:2]
    room = jnp.minimum(donor - 1, bound - receiver)
    moved = jax.random.randint(jax.random.fold_in(stream_key, 1), (couples,), 0, 1 << 20) % (room + 1)
    lengths = lengths.at[1:1 + 2 * couples:2].set(donor - moved).at[2:2 + 2 * couples:2].set(receiver + moved)
    return lengths[jax.random.permutation(jax.random.fold_in(stream_key, 2), amount)]


def normal_values(own_key, shape, spread, reach, shards=(), dtype=jnp.bfloat16):
    drawn = spread * jax.random.normal(own_key, shape, jnp.float32)
    if shards:
        drawn = drawn * levels(own_key, shape, shards, -0.22, 0.18)
    return jnp.clip(drawn, -reach, reach).astype(dtype)


def heavy_noise(rng, shape, deviation, bound, shards, heavy, kind=jnp.bfloat16):
    array = deviation * jax.random.normal(rng, shape, jnp.float32)
    if shards:
        array = array * levels(rng, shape, shards, -0.22, 0.18)
    return jnp.clip(raised(array, jax.random.fold_in(rng, 3), *heavy), -bound, bound).astype(kind)


def setup_inputs(seed: int = 0) -> dict:
    splits = jax.random.split(jax.random.key(seed), 7)
    return {
        "saved_inputs": heavy_noise(splits[0], (LAYERS, TOKENS, D), 1.0, 6.0, ((0, 8), (1, 16)), (1, 2, 16, 2.0)),
        "cotangent": normal_values(splits[1], (TOKENS, D), 1.0, 6.0, ((0, 16),)),
        "pack_lists": jax.vmap(lambda own: jax.random.permutation(own, TOK_DEV))(jax.random.split(splits[2], N_DP)).reshape((N_DP, TOK_DEV)).astype(jnp.int32),
        "segment_ids": jax.vmap(lambda own: jnp.searchsorted(jnp.cumsum(uneven_parts(own, SEQ_MAX, MB_ROWS, MB_ROWS // 2, 2)), jnp.arange(MB_ROWS), side="right"))(jax.random.split(splits[3], (TOKENS // MB_ROWS))).reshape((TOKENS // MB_ROWS, MB_ROWS)).astype(jnp.int32),
        "w_in": normal_values(splits[4], (LAYERS, D, 4 * D), D ** -0.5, 0.1875, ((0, 8),)),
        "w_out": normal_values(splits[5], (LAYERS, D, D), D ** -0.5, 0.1875, ((0, 8),)),
    }


def norm_rows(values):
    centered = values - lax.optimization_barrier(jnp.mean(values, axis=-1, keepdims=True))
    variance = lax.optimization_barrier(jnp.mean(centered * centered, axis=-1, keepdims=True))
    return centered * lax.rsqrt(variance + 1e-05)

def mixer(pre, segments):
    row_count = pre.shape[0]
    model_width = pre.shape[1] // 4
    head_dim = model_width // H
    active = jax.nn.silu(pre)
    gate_part = active[:, :model_width]
    value_part = active[:, model_width:2 * model_width].astype(jnp.bfloat16).reshape(row_count, H, head_dim)
    query_part = active[:, 2 * model_width:3 * model_width].astype(jnp.bfloat16).reshape(row_count, H, head_dim)
    key_part = active[:, 3 * model_width:].astype(jnp.bfloat16).reshape(row_count, H, head_dim)
    scores = jnp.einsum('ihd,jhd->hij', query_part, key_part, preferred_element_type=jnp.float32) / jnp.sqrt(jnp.float32(head_dim))
    positions = jnp.arange(row_count)
    allowed = (segments[:, None] == segments[None, :]) & (positions[None, :] <= positions[:, None])
    weights = (jax.nn.silu(scores) * allowed.astype(jnp.float32) / row_count).astype(jnp.bfloat16)
    mixed = jnp.einsum('hij,jhd->ihd', weights, value_part, preferred_element_type=jnp.float32).reshape(row_count, model_width)
    return norm_rows(mixed) * gate_part

def times_transpose(left, right):
    return lax.dot_general(left, right, (((1,), (1,)), ((), ())), preferred_element_type=jnp.float32)

def layer_grads(inputs_here, grad_here, segments, weight_in, weight_out):
    normed, norm_back = jax.vjp(norm_rows, inputs_here.astype(jnp.float32))
    normed_b = normed.astype(jnp.bfloat16)
    pre = jnp.dot(normed_b, weight_in, preferred_element_type=jnp.float32)
    mixed, mix_back = jax.vjp(lambda value_in: mixer(value_in, segments), pre)
    mixed_b = mixed.astype(jnp.bfloat16)
    grad_mixed = times_transpose(grad_here, weight_out).astype(jnp.bfloat16)
    grad_pre = mix_back(grad_mixed.astype(jnp.float32))[0].astype(jnp.bfloat16)
    grad_normed = times_transpose(grad_pre, weight_in)
    grad_x = (grad_here.astype(jnp.float32) + norm_back(grad_normed)[0]).astype(jnp.bfloat16)
    return (grad_x, normed_b, grad_pre, mixed_b)

def contract_rows(left, right):
    return lax.dot_general(left, right, (((0,), (0,)), ((), ())), preferred_element_type=jnp.float32)

def reference(saved_inputs, cotangent, pack_lists, segment_ids, w_in, w_out):
    share = TOK_DEV // N_DP
    loader = cotangent.reshape(N_DP, TOK_DEV, D)
    picked = loader[jnp.arange(N_DP)[:, None], pack_lists]
    packed = picked.reshape(N_DP, N_DP, share, D).transpose(1, 0, 2, 3).reshape(TOKENS, D)
    batches = TOKENS // MB_ROWS
    grad_here = packed.reshape(batches, MB_ROWS, D)
    input_grads = []
    in_grads = []
    out_grads = []
    for layer in range(N_SECTION - 1, -1, -1):
        inputs_here = saved_inputs[layer].reshape(batches, MB_ROWS, D)
        grad_x, normed_b, grad_pre, mixed_b = jax.vmap(layer_grads, in_axes=(0, 0, 0, None, None))(inputs_here, grad_here, segment_ids, w_in[layer], w_out[layer])
        in_grads.append(contract_rows(normed_b.reshape(TOKENS, D), grad_pre.reshape(TOKENS, 4 * D)))
        out_grads.append(contract_rows(mixed_b.reshape(TOKENS, D), grad_here.reshape(TOKENS, D)))
        input_grads.append(grad_x.reshape(TOKENS, D))
        grad_here = grad_x
    grad_inputs = jnp.stack(input_grads[::-1])
    grad_w_in = jnp.stack(in_grads[::-1])
    grad_w_out = jnp.stack(out_grads[::-1])
    return (grad_inputs, grad_w_in, grad_w_out)
```

```python
import jax
import jax.numpy as jnp
from jax import lax
from jax.experimental import pallas as pl
from jax.experimental.pallas import tpu as pltpu
from jax.sharding import PartitionSpec as P

H = 16
HEAD = 64
MB = 64
WIDE = 256
GROUP = WIDE // HEAD
EPS = 1e-05
SKEW_NEAR = 1
SKEW_FAR = 3
MIB = 1 << 20
VMEM = pltpu.VMEM
F32 = jnp.float32
BF16 = jnp.bfloat16


def whole(count):
    return [pl.BlockSpec(memory_space=VMEM)] * count


def dot_nn(left, right):
    return lax.dot_general(left, right, (((1,), (0,)), ((), ())), preferred_element_type=F32)


def dot_nt(left, right):
    return lax.dot_general(left, right, (((1,), (1,)), ((), ())), preferred_element_type=F32)


def dot_tn(left, right):
    return lax.dot_general(left, right, (((0,), (0,)), ((), ())), preferred_element_type=F32)


def head_masks():
    lane = lax.broadcasted_iota(jnp.int32, (MB, WIDE), 1)
    return [((lane >= h * HEAD) & (lane < (h + 1) * HEAD)) for h in range(GROUP)]


def spread(block, masks):
    wide = block.astype(F32)
    return jnp.concatenate([jnp.where(m, wide, 0.0).astype(BF16) for m in masks], axis=0)


def gather_heads(full, masks):
    total = jnp.where(masks[0], full[:MB], 0.0)
    for h in range(1, GROUP):
        total = jnp.where(masks[h], full[h * MB : (h + 1) * MB], total)
    return total


def mean_rows(values):
    return jnp.sum(values, axis=-1, keepdims=True) * (1.0 / values.shape[-1])


def forward_kernel(
    x_ref, mask_ref, win_ref,
    q_ref, k_ref, v_ref, gate_ref, n2_ref, att_ref, ds_ref, dsil_ref, xn_ref, xnt_ref, yut_ref,
    r1_ref, r2_ref, mixed,
):
    rows = x_ref.shape[0]
    width = x_ref.shape[1]
    block = 4 * MB
    masks = head_masks()

    def row_block(rb, carry):
        r0 = pl.multiple_of(rb * block, block)
        here = pl.ds(r0, block)
        x = x_ref[here, :].astype(F32)
        centered = x - mean_rows(x)
        r1 = lax.rsqrt(mean_rows(centered * centered) + EPS)
        xn = (centered * r1).astype(BF16)
        xn_ref[here, :] = xn
        r1_ref[here, :] = jnp.broadcast_to(r1, (block, 128))

        def col_block(cb, carry2):
            outs = (gate_ref, v_ref, q_ref, k_ref)
            cols = pl.ds(pl.multiple_of(cb * WIDE, WIDE), WIDE)
            for part in range(4):
                wide = pl.ds(pl.multiple_of(part * width + cb * WIDE, WIDE), WIDE)
                pre = dot_nn(xn_ref[here, :], win_ref[:, wide])
                sig = jax.nn.sigmoid(pre)
                act = pre * sig
                outs[part][here, cols] = act.astype(BF16)
                dsil_ref[here, wide] = (sig + act * (1.0 - sig)).astype(BF16)
            for m in range(4):
                rr = pl.ds(pl.multiple_of(r0 + m * MB, MB), MB)
                k4 = spread(k_ref[rr, cols], masks)
                v4 = spread(v_ref[rr, cols], masks)
                s = dot_nt(q_ref[rr, cols], k4) * (1.0 / 8.0)
                mask = mask_ref[rr, :]
                sg = jax.nn.sigmoid(s)
                sil = s * sg
                att = (sil * mask * (1.0 / MB)).astype(BF16)
                att_ref[rr, cols] = att
                ds_ref[rr, cols] = ((sg + sil * (1.0 - sg)) * mask * (1.0 / (8 * MB))).astype(BF16)
                mixed[m * MB : (m + 1) * MB, cols] = dot_nn(att, v4)
            return carry2

        lax.fori_loop(0, width // WIDE, col_block, 0)
        mx = mixed[...]
        cm = mx - mean_rows(mx)
        r2 = lax.rsqrt(mean_rows(cm * cm) + EPS)
        r2_ref[here, :] = jnp.broadcast_to(r2, (block, 128))
        n2 = cm * r2
        n2_ref[here, :] = n2.astype(BF16)
        mixed[...] = n2 * gate_ref[here, :].astype(F32)
        return carry

    lax.fori_loop(0, rows // block, row_block, 0)


def transpose_kernel(xn_ref, n2_ref, gate_ref, xnt_ref, yut_ref):
    xnt_ref[...] = xn_ref[...].T
    yu = n2_ref[...].astype(F32) * gate_ref[...].astype(F32)
    yut_ref[...] = yu.astype(BF16).T


def forward(x, mask, win):
    rows, width = x.shape
    small = jax.ShapeDtypeStruct((rows, width), BF16)
    big = jax.ShapeDtypeStruct((rows, 4 * width), BF16)
    turned = jax.ShapeDtypeStruct((width, rows), BF16)
    stat = jax.ShapeDtypeStruct((rows, 128), F32)

    def run(x_ref, mask_ref, win_ref, q, k, v, gate, n2, att, ds, dsil, xn, r1, r2, mixed):
        forward_kernel(
            x_ref, mask_ref, win_ref, q, k, v, gate, n2, att, ds, dsil, xn, None, None, r1, r2, mixed
        )

    q, k, v, gate, n2, att, ds, dsil, xn, r1, r2 = pl.pallas_call(
        run,
        out_shape=(small,) * 7 + (big, small, stat, stat),
        in_specs=whole(3),
        out_specs=tuple(whole(11)),
        scratch_shapes=[pltpu.VMEM((4 * MB, width), F32)],
        compiler_params=pltpu.CompilerParams(vmem_limit_bytes=12 * MIB),
        name="forward",
    )(x, mask, win)
    keep = lambda a: pltpu.with_memory_space_constraint(a, VMEM)
    q, k, v, gate, n2, att, ds, dsil, xn, r1, r2 = [
        keep(a) for a in (q, k, v, gate, n2, att, ds, dsil, xn, r1, r2)
    ]
    xnt, yut = pl.pallas_call(
        transpose_kernel,
        out_shape=(turned, turned),
        in_specs=whole(3),
        out_specs=tuple(whole(2)),
        compiler_params=pltpu.CompilerParams(vmem_limit_bytes=12 * MIB),
        name="turn",
    )(xn, n2, gate)
    return q, k, v, gate, n2, att, ds, dsil, xn, keep(xnt), keep(yut), r1, r2


def step_kernel(
    sc_ref, packed_ref, near_ref, far_ref, win_ref, wout_ref, q_ref, k_ref, v_ref, gate_ref, n2_ref, att_ref,
    ds_ref, xn_ref, r1_ref, r2_ref, dpre_in, gall_in, dxall_in,
    out_ref, dpre_ref, gall_ref, dxall_ref, gbuf,
):
    slot, valid, source = sc_ref[0], sc_ref[1], sc_ref[2]
    width = out_ref.shape[1]

    @pl.when(valid == 1)
    def _():
        rr = pl.ds(pl.multiple_of(slot * MB, MB), MB)

        @pl.when(source == 0)
        def _():
            gbuf[...] = packed_ref[rr, :]

        @pl.when(source == 1)
        def _():
            gbuf[...] = near_ref[...]

        @pl.when(source == 2)
        def _():
            gbuf[...] = far_ref[...]

        masks = head_masks()
        g = gbuf[...]
        gall_ref[rr, :] = g
        d_yu = dot_nt(g, wout_ref[...]).astype(BF16).astype(F32)
        n2 = n2_ref[rr, :].astype(F32)
        gate = gate_ref[rr, :].astype(F32)
        d_gate = d_yu * n2
        d_n2 = d_yu * gate
        r2 = r2_ref[rr, :][:, :1]
        d_mixed = (r2 * (d_n2 - mean_rows(d_n2) - n2 * mean_rows(d_n2 * n2))).astype(BF16)
        dpre_ref[rr, :width] = (d_gate * dpre_in[rr, :width].astype(F32)).astype(BF16)
        for c in range(width // WIDE):
            lo = c * WIDE
            do4 = d_mixed[:, lo : lo + WIDE]
            q4 = q_ref[rr, lo : lo + WIDE]
            k4 = spread(k_ref[rr, lo : lo + WIDE], masks)
            v4 = spread(v_ref[rr, lo : lo + WIDE], masks)
            att = att_ref[rr, lo : lo + WIDE]
            d_att = dot_nt(do4, v4)
            d_s = (d_att * ds_ref[rr, lo : lo + WIDE].astype(F32)).astype(BF16)
            d_q = dot_nn(d_s, k4)
            d_k = gather_heads(dot_tn(d_s, q4), masks)
            d_v = gather_heads(dot_tn(att, do4), masks)
            for part, val in ((1, d_v), (2, d_q), (3, d_k)):
                at = part * width + lo
                dpre_ref[rr, at : at + WIDE] = (
                    val * dpre_in[rr, at : at + WIDE].astype(F32)
                ).astype(BF16)
        d_xn = dot_nt(dpre_ref[rr, :], win_ref[...])
        xn = xn_ref[rr, :].astype(F32)
        r1 = r1_ref[rr, :][:, :1]
        dx = g.astype(F32) + r1 * (d_xn - mean_rows(d_xn) - xn * mean_rows(d_xn * xn))
        dx = dx.astype(BF16)
        out_ref[...] = dx
        dxall_ref[rr, :] = dx


def step(sc, packed, near, far, win, wout, saved, dpre, gall, dxall):
    q, k, v, gate, n2, att, ds, xn, r1, r2 = saved
    width = q.shape[1]
    return pl.pallas_call(
        step_kernel,
        out_shape=(
            jax.ShapeDtypeStruct((MB, width), BF16),
            jax.ShapeDtypeStruct(dpre.shape, BF16),
            jax.ShapeDtypeStruct(gall.shape, BF16),
            jax.ShapeDtypeStruct(dxall.shape, BF16),
        ),
        in_specs=[pl.BlockSpec(memory_space=pltpu.SMEM)] + whole(18),
        out_specs=tuple(whole(4)),
        input_output_aliases={16: 1, 17: 2, 18: 3},
        scratch_shapes=[pltpu.VMEM((MB, width), BF16)],
        compiler_params=pltpu.CompilerParams(vmem_limit_bytes=8 * MIB),
        name="step",
    )(sc, packed, near, far, win, wout, q, k, v, gate, n2, att, ds, xn, r1, r2, dpre, gall, dxall)


def weights_kernel(xnt_ref, yut_ref, dpre_ref, gall_ref, out_ref):
    width = gall_ref.shape[1]
    block = 512

    def body(i, carry):
        cols = pl.ds(pl.multiple_of(i * block, block), block)
        out_ref[:, cols] = dot_nn(xnt_ref[...], dpre_ref[:, cols]).astype(BF16)
        return carry

    lax.fori_loop(0, 4 * width // block, body, 0)

    def body2(i, carry):
        cols = pl.ds(pl.multiple_of(i * block, block), block)
        there = pl.ds(pl.multiple_of(4 * width + i * block, block), block)
        out_ref[:, there] = dot_nn(yut_ref[...], gall_ref[:, cols]).astype(BF16)
        return carry

    lax.fori_loop(0, width // block, body2, 0)


def body(saved_inputs, cotangent, pack_lists, segment_ids, w_in, w_out):
    dp_count = lax.axis_size("dp")
    section_count = lax.axis_size("section")
    section_index = lax.axis_index("section")
    tok_rows, width = cotangent.shape
    micro_count, mb_rows = segment_ids.shape
    share = tok_rows // dp_count
    keep = lambda a: pltpu.with_memory_space_constraint(a, VMEM)
    picked = cotangent[pack_lists[0]]
    packed = lax.all_to_all(
        picked.reshape(dp_count, share, width), "dp", split_axis=0, concat_axis=0, tiled=True
    ).reshape(tok_rows, width)
    win = keep(w_in[0])
    wout = keep(w_out[0])
    tiled = jnp.tile(segment_ids, (1, GROUP))
    pos = jnp.arange(mb_rows)
    allowed = (segment_ids[:, :, None] == tiled[:, None, :]) & (
        (jnp.arange(WIDE) % mb_rows)[None, None, :] <= pos[None, :, None]
    )
    mask = allowed.astype(F32).reshape(tok_rows, WIDE)
    q, k, v, gate, n2, att, ds, dpre, xn, xnt, yut, r1, r2 = forward(saved_inputs[0], mask, win)
    saved = (q, k, v, gate, n2, att, ds, xn, r1, r2)

    hops = section_count - 1
    lag = lambda h: SKEW_NEAR * ((h + 1) // 2) + SKEW_FAR * (h // 2)
    steps = micro_count + lag(hops)
    slots = jnp.arange(steps, dtype=jnp.int32) - lag(hops - section_index).astype(jnp.int32)
    valid = ((slots >= 0) & (slots < micro_count)).astype(jnp.int32)
    first = section_index == hops
    source = jnp.where(first, 0, jnp.where(section_index % 2 == 0, 1, 2)).astype(jnp.int32)
    table = jnp.stack(
        [jnp.clip(slots, 0, micro_count - 1), valid, jnp.broadcast_to(source, slots.shape)], axis=1
    )
    near_perm = [(s, s - 1) for s in range(1, section_count, 2)]
    far_perm = [(s, s - 1) for s in range(2, section_count, 2)]

    packed = keep(packed)
    zero = jnp.zeros((mb_rows, width), BF16)
    nears, fars = {}, {}
    gall = keep(jnp.zeros((tok_rows, width), BF16))
    dxall = keep(jnp.zeros((tok_rows, width), BF16))
    for t in range(steps):
        near = nears.pop(t - SKEW_NEAR, zero)
        far = fars.pop(t - SKEW_FAR, zero)
        dx, dpre, gall, dxall = step(table[t], packed, near, far, win, wout, saved, dpre, gall, dxall)
        if t + SKEW_NEAR < steps:
            nears[t] = lax.ppermute(dx, "section", near_perm)
        if t + SKEW_FAR < steps:
            fars[t] = lax.ppermute(dx, "section", far_perm)

    store = pl.pallas_call(
        weights_kernel,
        out_shape=jax.ShapeDtypeStruct((width, 5 * width), BF16),
        in_specs=whole(4),
        out_specs=pl.BlockSpec(memory_space=VMEM),
        compiler_params=pltpu.CompilerParams(vmem_limit_bytes=8 * MIB),
        name="weights",
    )(xnt, yut, dpre, gall)
    summed = lax.psum_scatter(store, "dp", scatter_dimension=0, tiled=True).astype(F32)
    return (dxall[None], summed[:, : 4 * width][None], summed[:, 4 * width :][None])


def solution(mesh):
    return jax.shard_map(
        body,
        mesh=mesh,
        in_specs=(
            P("section", "dp", None),
            P("dp", None),
            P("dp", None),
            P("dp", None),
            P("section", None, None),
            P("section", None, None),
        ),
        out_specs=(P("section", "dp", None), P("section", "dp", None), P("section", "dp", None)),
        check_vma=False,
    )
```

```python
import jax
import jax.numpy as jnp
from jax import lax
from jax.experimental import pallas as pl
from jax.experimental.pallas import tpu as pltpu
from jax.sharding import PartitionSpec as P

H = 16
HEAD = 64
MB = 64
WIDE = 256
GROUP = WIDE // HEAD
EPS = 1e-05
SKEW_NEAR = 1
SKEW_FAR = 2
ROWS = 2 * MB
MIB = 1 << 20
VMEM = pltpu.VMEM
F32 = jnp.float32
BF16 = jnp.bfloat16


def whole(count):
    return [pl.BlockSpec(memory_space=VMEM)] * count


def dot_nn(left, right):
    return lax.dot_general(left, right, (((1,), (0,)), ((), ())), preferred_element_type=F32)


def dot_nt(left, right):
    return lax.dot_general(left, right, (((1,), (1,)), ((), ())), preferred_element_type=F32)


def dot_tn(left, right):
    return lax.dot_general(left, right, (((0,), (0,)), ((), ())), preferred_element_type=F32)


def head_masks():
    lane = lax.broadcasted_iota(jnp.int32, (MB, WIDE), 1)
    return [((lane >= h * HEAD) & (lane < (h + 1) * HEAD)) for h in range(GROUP)]


def spread(block, masks):
    wide = block.astype(F32)
    return jnp.concatenate([jnp.where(m, wide, 0.0).astype(BF16) for m in masks], axis=0)


def gather_heads(full, masks):
    total = jnp.where(masks[0], full[:MB], 0.0)
    for h in range(1, GROUP):
        total = jnp.where(masks[h], full[h * MB : (h + 1) * MB], total)
    return total


def mean_rows(values):
    return jnp.sum(values, axis=-1, keepdims=True) * (1.0 / values.shape[-1])


def forward_kernel(
    x_ref, mask_ref, win_ref,
    q_ref, k_ref, v_ref, gate_ref, n2_ref, att_ref, ds_ref, dsil_ref, xn_ref, xnt_ref, yut_ref,
    r1_ref, r2_ref, mixed,
):
    rows = x_ref.shape[0]
    width = x_ref.shape[1]
    block = 4 * MB
    masks = head_masks()

    def row_block(rb, carry):
        r0 = pl.multiple_of(rb * block, block)
        here = pl.ds(r0, block)
        x = x_ref[here, :].astype(F32)
        centered = x - mean_rows(x)
        r1 = lax.rsqrt(mean_rows(centered * centered) + EPS)
        xn = (centered * r1).astype(BF16)
        xn_ref[here, :] = xn
        r1_ref[here, :] = jnp.broadcast_to(r1, (block, 128))

        def col_block(cb, carry2):
            outs = (gate_ref, v_ref, q_ref, k_ref)
            cols = pl.ds(pl.multiple_of(cb * WIDE, WIDE), WIDE)
            for part in range(4):
                wide = pl.ds(pl.multiple_of(part * width + cb * WIDE, WIDE), WIDE)
                pre = dot_nn(xn_ref[here, :], win_ref[:, wide])
                sig = jax.nn.sigmoid(pre)
                act = pre * sig
                outs[part][here, cols] = act.astype(BF16)
                dsil_ref[here, wide] = (sig + act * (1.0 - sig)).astype(BF16)
            for m in range(4):
                rr = pl.ds(pl.multiple_of(r0 + m * MB, MB), MB)
                k4 = spread(k_ref[rr, cols], masks)
                v4 = spread(v_ref[rr, cols], masks)
                s = dot_nt(q_ref[rr, cols], k4) * (1.0 / 8.0)
                mask = mask_ref[rr, :]
                sg = jax.nn.sigmoid(s)
                sil = s * sg
                att = (sil * mask * (1.0 / MB)).astype(BF16)
                att_ref[rr, cols] = att
                ds_ref[rr, cols] = ((sg + sil * (1.0 - sg)) * mask * (1.0 / (8 * MB))).astype(BF16)
                mixed[m * MB : (m + 1) * MB, cols] = dot_nn(att, v4)
            return carry2

        lax.fori_loop(0, width // WIDE, col_block, 0)
        mx = mixed[...]
        cm = mx - mean_rows(mx)
        r2 = lax.rsqrt(mean_rows(cm * cm) + EPS)
        r2_ref[here, :] = jnp.broadcast_to(r2, (block, 128))
        n2 = cm * r2
        n2_ref[here, :] = n2.astype(BF16)
        mixed[...] = n2 * gate_ref[here, :].astype(F32)
        return carry

    lax.fori_loop(0, rows // block, row_block, 0)


def transpose_kernel(xn_ref, n2_ref, gate_ref, xnt_ref, yut_ref):
    xnt_ref[...] = xn_ref[...].T
    yu = n2_ref[...].astype(F32) * gate_ref[...].astype(F32)
    yut_ref[...] = yu.astype(BF16).T


def forward(x, mask, win):
    rows, width = x.shape
    small = jax.ShapeDtypeStruct((rows, width), BF16)
    big = jax.ShapeDtypeStruct((rows, 4 * width), BF16)
    turned = jax.ShapeDtypeStruct((width, rows), BF16)
    stat = jax.ShapeDtypeStruct((rows, 128), F32)

    def run(x_ref, mask_ref, win_ref, q, k, v, gate, n2, att, ds, dsil, xn, r1, r2, mixed):
        forward_kernel(
            x_ref, mask_ref, win_ref, q, k, v, gate, n2, att, ds, dsil, xn, None, None, r1, r2, mixed
        )

    q, k, v, gate, n2, att, ds, dsil, xn, r1, r2 = pl.pallas_call(
        run,
        out_shape=(small,) * 7 + (big, small, stat, stat),
        in_specs=whole(3),
        out_specs=tuple(whole(11)),
        scratch_shapes=[pltpu.VMEM((4 * MB, width), F32)],
        compiler_params=pltpu.CompilerParams(vmem_limit_bytes=8 * MIB),
        name="forward",
    )(x, mask, win)
    xnt, yut = pl.pallas_call(
        transpose_kernel,
        out_shape=(turned, turned),
        in_specs=whole(3),
        out_specs=tuple(whole(2)),
        compiler_params=pltpu.CompilerParams(vmem_limit_bytes=8 * MIB),
        name="turn",
    )(xn, n2, gate)
    return q, k, v, gate, n2, att, ds, dsil, xn, xnt, yut, r1, r2


def step_kernel(
    sc_ref, packed_ref, near_ref, far_ref, win_ref, wout_ref, q_ref, k_ref, v_ref, gate_ref, n2_ref, att_ref,
    ds_ref, xn_ref, r1_ref, r2_ref, dpre_in, gall_in, dxall_in,
    out_ref, dpre_ref, gall_ref, dxall_ref, gbuf,
):
    slot, valid, source = sc_ref[0], sc_ref[1], sc_ref[2]
    width = out_ref.shape[1]

    @pl.when(valid == 1)
    def _():
        rr = pl.ds(pl.multiple_of(slot * ROWS, ROWS), ROWS)

        @pl.when(source == 0)
        def _():
            gbuf[...] = packed_ref[rr, :]

        @pl.when(source == 1)
        def _():
            gbuf[...] = near_ref[...]

        @pl.when(source == 2)
        def _():
            gbuf[...] = far_ref[...]

        masks = head_masks()
        g = gbuf[...]
        gall_ref[rr, :] = g
        d_yu = dot_nn(g, wout_ref[...]).astype(BF16).astype(F32)
        n2 = n2_ref[rr, :].astype(F32)
        gate = gate_ref[rr, :].astype(F32)
        d_gate = d_yu * n2
        d_n2 = d_yu * gate
        r2 = r2_ref[rr, :][:, :1]
        d_mixed = (r2 * (d_n2 - mean_rows(d_n2) - n2 * mean_rows(d_n2 * n2))).astype(BF16)
        dpre_ref[rr, :width] = (d_gate * dpre_in[rr, :width].astype(F32)).astype(BF16)
        for c in range(width // WIDE):
            lo = c * WIDE
            cols = slice(lo, lo + WIDE)
            for m in range(ROWS // MB):
                mm = pl.ds(pl.multiple_of(slot * ROWS + m * MB, MB), MB)
                do4 = d_mixed[m * MB : (m + 1) * MB, cols]
                q4 = q_ref[mm, cols]
                k4 = spread(k_ref[mm, cols], masks)
                v4 = spread(v_ref[mm, cols], masks)
                att = att_ref[mm, cols]
                d_att = dot_nt(do4, v4)
                d_s = (d_att * ds_ref[mm, cols].astype(F32)).astype(BF16)
                d_q = dot_nn(d_s, k4)
                d_k = gather_heads(dot_tn(d_s, q4), masks)
                d_v = gather_heads(dot_tn(att, do4), masks)
                for part, val in ((1, d_v), (2, d_q), (3, d_k)):
                    at = slice(part * width + lo, part * width + lo + WIDE)
                    dpre_ref[mm, at] = (val * dpre_in[mm, at].astype(F32)).astype(BF16)
        d_xn = dot_nn(dpre_ref[rr, :], win_ref[...])
        xn = xn_ref[rr, :].astype(F32)
        r1 = r1_ref[rr, :][:, :1]
        dx = g.astype(F32) + r1 * (d_xn - mean_rows(d_xn) - xn * mean_rows(d_xn * xn))
        dx = dx.astype(BF16)
        out_ref[...] = dx
        dxall_ref[rr, :] = dx


def turn_weights_kernel(win_ref, wout_ref, wint_ref, woutt_ref):
    wint_ref[...] = win_ref[...].T
    woutt_ref[...] = wout_ref[...].T


def turn_weights(win, wout):
    shapes = [jax.ShapeDtypeStruct(w.shape[::-1], BF16) for w in (win, wout)]
    return pl.pallas_call(
        turn_weights_kernel,
        out_shape=tuple(shapes),
        in_specs=whole(2),
        out_specs=tuple(whole(2)),
        compiler_params=pltpu.CompilerParams(vmem_limit_bytes=4 * MIB),
        name="turn_weights",
    )(win, wout)


def step(sc, packed, near, far, win, wout, saved, dpre, gall, dxall):
    q, k, v, gate, n2, att, ds, xn, r1, r2 = saved
    width = q.shape[1]
    return pl.pallas_call(
        step_kernel,
        out_shape=(
            jax.ShapeDtypeStruct((ROWS, width), BF16),
            jax.ShapeDtypeStruct(dpre.shape, BF16),
            jax.ShapeDtypeStruct(gall.shape, BF16),
            jax.ShapeDtypeStruct(dxall.shape, BF16),
        ),
        in_specs=[pl.BlockSpec(memory_space=pltpu.SMEM)] + whole(18),
        out_specs=tuple(whole(4)),
        input_output_aliases={16: 1, 17: 2, 18: 3},
        scratch_shapes=[pltpu.VMEM((ROWS, width), BF16)],
        compiler_params=pltpu.CompilerParams(vmem_limit_bytes=8 * MIB),
        name="step",
    )(sc, packed, near, far, win, wout, q, k, v, gate, n2, att, ds, xn, r1, r2, dpre, gall, dxall)


def weights_kernel(xnt_ref, yut_ref, dpre_ref, gall_ref, out_ref):
    width = gall_ref.shape[1]
    block = 512

    def body(i, carry):
        cols = pl.ds(pl.multiple_of(i * block, block), block)
        out_ref[:, cols] = dot_nn(xnt_ref[...], dpre_ref[:, cols]).astype(BF16)
        return carry

    lax.fori_loop(0, 4 * width // block, body, 0)

    def body2(i, carry):
        cols = pl.ds(pl.multiple_of(i * block, block), block)
        there = pl.ds(pl.multiple_of(4 * width + i * block, block), block)
        out_ref[:, there] = dot_nn(yut_ref[...], gall_ref[:, cols]).astype(BF16)
        return carry

    lax.fori_loop(0, width // block, body2, 0)


def body(saved_inputs, cotangent, pack_lists, segment_ids, w_in, w_out):
    dp_count = lax.axis_size("dp")
    section_count = lax.axis_size("section")
    section_index = lax.axis_index("section")
    tok_rows, width = cotangent.shape
    micro_count, mb_rows = segment_ids.shape
    share = tok_rows // dp_count
    picked = cotangent[pack_lists[0]]
    packed = lax.all_to_all(
        picked.reshape(dp_count, share, width), "dp", split_axis=0, concat_axis=0, tiled=True
    ).reshape(tok_rows, width)
    packed, saved_inputs, w_in, w_out = lax.optimization_barrier((packed, saved_inputs, w_in, w_out))
    tiled = jnp.tile(segment_ids, (1, GROUP))
    pos = jnp.arange(mb_rows)
    allowed = (segment_ids[:, :, None] == tiled[:, None, :]) & (
        (jnp.arange(WIDE) % mb_rows)[None, None, :] <= pos[None, :, None]
    )
    mask = allowed.astype(F32).reshape(tok_rows, WIDE)
    q, k, v, gate, n2, att, ds, dpre, xn, xnt, yut, r1, r2 = forward(saved_inputs[0], mask, w_in[0])
    saved = (q, k, v, gate, n2, att, ds, xn, r1, r2)
    win, wout = turn_weights(w_in[0], w_out[0])

    hops = section_count - 1
    lag = lambda h: SKEW_NEAR * ((h + 1) // 2) + SKEW_FAR * (h // 2)
    chunks = tok_rows // ROWS
    steps = chunks + lag(hops)
    slots = jnp.arange(steps, dtype=jnp.int32) - lag(hops - section_index).astype(jnp.int32)
    valid = ((slots >= 0) & (slots < chunks)).astype(jnp.int32)
    first = section_index == hops
    source = jnp.where(first, 0, jnp.where(section_index % 2 == 0, 1, 2)).astype(jnp.int32)
    table = jnp.stack(
        [jnp.clip(slots, 0, chunks - 1), valid, jnp.broadcast_to(source, slots.shape)], axis=1
    )
    near_perm = [(s, s - 1) for s in range(1, section_count, 2)]
    far_perm = [(s, s - 1) for s in range(2, section_count, 2)]

    zero = jnp.zeros((ROWS, width), BF16)
    nears, fars = {}, {}
    keep = lambda a: pltpu.with_memory_space_constraint(a, VMEM)
    dpre = keep(dpre)
    gall = keep(jnp.zeros((tok_rows, width), BF16))
    dxall = keep(jnp.zeros((tok_rows, width), BF16))
    for t in range(steps):
        near = nears.pop(t - SKEW_NEAR, zero)
        far = fars.pop(t - SKEW_FAR, zero)
        dx, dpre, gall, dxall = step(table[t], packed, near, far, win, wout, saved, dpre, gall, dxall)
        if t + SKEW_NEAR < steps:
            nears[t] = lax.ppermute(dx, "section", near_perm)
        if t + SKEW_FAR < steps:
            fars[t] = lax.ppermute(dx, "section", far_perm)

    store = pl.pallas_call(
        weights_kernel,
        out_shape=jax.ShapeDtypeStruct((width, 5 * width), BF16),
        in_specs=whole(4),
        out_specs=pl.BlockSpec(memory_space=VMEM),
        compiler_params=pltpu.CompilerParams(vmem_limit_bytes=8 * MIB),
        name="weights",
    )(xnt, yut, dpre, gall)
    summed = lax.psum_scatter(store, "dp", scatter_dimension=0, tiled=True).astype(F32)
    return (dxall[None], summed[:, : 4 * width][None], summed[:, 4 * width :][None])


def solution(mesh):
    return jax.shard_map(
        body,
        mesh=mesh,
        in_specs=(
            P("section", "dp", None),
            P("dp", None),
            P("dp", None),
            P("dp", None),
            P("section", None, None),
            P("section", None, None),
        ),
        out_specs=(P("section", "dp", None), P("section", "dp", None), P("section", "dp", None)),
        check_vma=False,
    )
```

```python
import jax
import jax.numpy as jnp
from jax import lax
from jax.experimental import pallas as pl
from jax.experimental.pallas import tpu as pltpu
from jax.sharding import PartitionSpec as P

H = 16
HEAD = 64
MB = 64
WIDE = 256
GROUP = WIDE // HEAD
EPS = 1e-05
SKEW_NEAR = 1
SKEW_FAR = 2
ROWS = 2 * MB
MIB = 1 << 20
VMEM = pltpu.VMEM
F32 = jnp.float32
BF16 = jnp.bfloat16


def whole(count):
    return [pl.BlockSpec(memory_space=VMEM)] * count


def dot_nn(left, right):
    return lax.dot_general(left, right, (((1,), (0,)), ((), ())), preferred_element_type=F32)


def dot_nt(left, right):
    return lax.dot_general(left, right, (((1,), (1,)), ((), ())), preferred_element_type=F32)


def dot_tn(left, right):
    return lax.dot_general(left, right, (((0,), (0,)), ((), ())), preferred_element_type=F32)


def head_masks():
    lane = lax.broadcasted_iota(jnp.int32, (MB, WIDE), 1)
    return [((lane >= h * HEAD) & (lane < (h + 1) * HEAD)) for h in range(GROUP)]


def spread(block, masks):
    wide = block.astype(F32)
    return jnp.concatenate([jnp.where(m, wide, 0.0).astype(BF16) for m in masks], axis=0)


def gather_heads(full, masks):
    total = jnp.where(masks[0], full[:MB], 0.0)
    for h in range(1, GROUP):
        total = jnp.where(masks[h], full[h * MB : (h + 1) * MB], total)
    return total


def mean_rows(values):
    return jnp.sum(values, axis=-1, keepdims=True) * (1.0 / values.shape[-1])


def forward_kernel(
    x_ref, mask_ref, win_ref,
    q_ref, k_ref, v_ref, gate_ref, n2_ref, att_ref, ds_ref, dsil_ref, xn_ref, xnt_ref, yut_ref,
    r1_ref, r2_ref, mixed,
):
    rows = x_ref.shape[0]
    width = x_ref.shape[1]
    block = 4 * MB
    masks = head_masks()

    def row_block(rb, carry):
        r0 = pl.multiple_of(rb * block, block)
        here = pl.ds(r0, block)
        x = x_ref[here, :].astype(F32)
        centered = x - mean_rows(x)
        r1 = lax.rsqrt(mean_rows(centered * centered) + EPS)
        xn = (centered * r1).astype(BF16)
        xn_ref[here, :] = xn
        r1_ref[here, :] = jnp.broadcast_to(r1, (block, 128))

        def col_block(cb, carry2):
            outs = (gate_ref, v_ref, q_ref, k_ref)
            cols = pl.ds(pl.multiple_of(cb * WIDE, WIDE), WIDE)
            for part in range(4):
                wide = pl.ds(pl.multiple_of(part * width + cb * WIDE, WIDE), WIDE)
                pre = dot_nn(xn_ref[here, :], win_ref[:, wide])
                sig = jax.nn.sigmoid(pre)
                act = pre * sig
                outs[part][here, cols] = act.astype(BF16)
                dsil_ref[here, wide] = (sig + act * (1.0 - sig)).astype(BF16)
            for m in range(4):
                rr = pl.ds(pl.multiple_of(r0 + m * MB, MB), MB)
                k4 = spread(k_ref[rr, cols], masks)
                v4 = spread(v_ref[rr, cols], masks)
                s = dot_nt(q_ref[rr, cols], k4) * (1.0 / 8.0)
                mask = mask_ref[rr, :]
                sg = jax.nn.sigmoid(s)
                sil = s * sg
                att = (sil * mask * (1.0 / MB)).astype(BF16)
                att_ref[rr, cols] = att
                ds_ref[rr, cols] = ((sg + sil * (1.0 - sg)) * mask * (1.0 / (8 * MB))).astype(BF16)
                mixed[m * MB : (m + 1) * MB, cols] = dot_nn(att, v4)
            return carry2

        lax.fori_loop(0, width // WIDE, col_block, 0, unroll=True)
        mx = mixed[...]
        cm = mx - mean_rows(mx)
        r2 = lax.rsqrt(mean_rows(cm * cm) + EPS)
        r2_ref[here, :] = jnp.broadcast_to(r2, (block, 128))
        n2 = cm * r2
        n2_ref[here, :] = n2.astype(BF16)
        mixed[...] = n2 * gate_ref[here, :].astype(F32)
        return carry

    lax.fori_loop(0, rows // block, row_block, 0)


def transpose_kernel(xn_ref, n2_ref, gate_ref, xnt_ref, yut_ref):
    xnt_ref[...] = xn_ref[...].T
    yu = n2_ref[...].astype(F32) * gate_ref[...].astype(F32)
    yut_ref[...] = yu.astype(BF16).T


def forward(x, mask, win):
    rows, width = x.shape
    small = jax.ShapeDtypeStruct((rows, width), BF16)
    big = jax.ShapeDtypeStruct((rows, 4 * width), BF16)
    turned = jax.ShapeDtypeStruct((width, rows), BF16)
    stat = jax.ShapeDtypeStruct((rows, 128), F32)

    def run(x_ref, mask_ref, win_ref, q, k, v, gate, n2, att, ds, dsil, xn, r1, r2, mixed):
        forward_kernel(
            x_ref, mask_ref, win_ref, q, k, v, gate, n2, att, ds, dsil, xn, None, None, r1, r2, mixed
        )

    q, k, v, gate, n2, att, ds, dsil, xn, r1, r2 = pl.pallas_call(
        run,
        out_shape=(small,) * 7 + (big, small, stat, stat),
        in_specs=whole(3),
        out_specs=tuple(whole(11)),
        scratch_shapes=[pltpu.VMEM((4 * MB, width), F32)],
        compiler_params=pltpu.CompilerParams(vmem_limit_bytes=8 * MIB),
        name="forward",
    )(x, mask, win)
    xnt, yut = pl.pallas_call(
        transpose_kernel,
        out_shape=(turned, turned),
        in_specs=whole(3),
        out_specs=tuple(whole(2)),
        compiler_params=pltpu.CompilerParams(vmem_limit_bytes=8 * MIB),
        name="turn",
    )(xn, n2, gate)
    return q, k, v, gate, n2, att, ds, dsil, xn, xnt, yut, r1, r2


def step_kernel(
    sc_ref, packed_ref, near_ref, far_ref, win_ref, wout_ref, q_ref, k_ref, v_ref, gate_ref, n2_ref, att_ref,
    ds_ref, xn_ref, r1_ref, r2_ref, dpre_in, gall_in, dxall_in,
    out_ref, dpre_ref, gall_ref, dxall_ref, gbuf,
):
    slot, valid, source = sc_ref[0], sc_ref[1], sc_ref[2]
    width = out_ref.shape[1]

    @pl.when(valid == 1)
    def _():
        rr = pl.ds(pl.multiple_of(slot * ROWS, ROWS), ROWS)

        @pl.when(source == 0)
        def _():
            gbuf[...] = packed_ref[pl.ds(pl.multiple_of(sc_ref[3], 16), ROWS), :]

        @pl.when(source == 1)
        def _():
            gbuf[...] = near_ref[...]

        @pl.when(source == 2)
        def _():
            gbuf[...] = far_ref[...]

        masks = head_masks()
        g = gbuf[...]
        gall_ref[rr, :] = g
        d_yu = dot_nn(g, wout_ref[...]).astype(BF16).astype(F32)
        n2 = n2_ref[rr, :].astype(F32)
        gate = gate_ref[rr, :].astype(F32)
        d_gate = d_yu * n2
        d_n2 = d_yu * gate
        r2 = r2_ref[rr, :][:, :1]
        d_mixed = (r2 * (d_n2 - mean_rows(d_n2) - n2 * mean_rows(d_n2 * n2))).astype(BF16)
        dpre_ref[rr, :width] = (d_gate * dpre_in[rr, :width].astype(F32)).astype(BF16)
        for c in range(width // WIDE):
            lo = c * WIDE
            cols = slice(lo, lo + WIDE)
            for m in range(ROWS // MB):
                mm = pl.ds(pl.multiple_of(slot * ROWS + m * MB, MB), MB)
                do4 = d_mixed[m * MB : (m + 1) * MB, cols]
                q4 = q_ref[mm, cols]
                k4 = spread(k_ref[mm, cols], masks)
                v4 = spread(v_ref[mm, cols], masks)
                att = att_ref[mm, cols]
                d_att = dot_nt(do4, v4)
                d_s = (d_att * ds_ref[mm, cols].astype(F32)).astype(BF16)
                d_q = dot_nn(d_s, k4)
                d_k = gather_heads(dot_tn(d_s, q4), masks)
                d_v = gather_heads(dot_tn(att, do4), masks)
                for part, val in ((1, d_v), (2, d_q), (3, d_k)):
                    at = slice(part * width + lo, part * width + lo + WIDE)
                    dpre_ref[mm, at] = (val * dpre_in[mm, at].astype(F32)).astype(BF16)
        d_xn = dot_nn(dpre_ref[rr, :], win_ref[...])
        xn = xn_ref[rr, :].astype(F32)
        r1 = r1_ref[rr, :][:, :1]
        dx = g.astype(F32) + r1 * (d_xn - mean_rows(d_xn) - xn * mean_rows(d_xn * xn))
        dx = dx.astype(BF16)
        out_ref[...] = dx
        dxall_ref[rr, :] = dx


def turn_weights_kernel(win_ref, wout_ref, wint_ref, woutt_ref):
    wint_ref[...] = win_ref[...].T
    woutt_ref[...] = wout_ref[...].T


def turn_weights(win, wout):
    shapes = [jax.ShapeDtypeStruct(w.shape[::-1], BF16) for w in (win, wout)]
    return pl.pallas_call(
        turn_weights_kernel,
        out_shape=tuple(shapes),
        in_specs=whole(2),
        out_specs=tuple(whole(2)),
        compiler_params=pltpu.CompilerParams(vmem_limit_bytes=4 * MIB),
        name="turn_weights",
    )(win, wout)


def step(sc, packed, near, far, win, wout, saved, dpre, gall, dxall):
    q, k, v, gate, n2, att, ds, xn, r1, r2 = saved
    width = q.shape[1]
    return pl.pallas_call(
        step_kernel,
        out_shape=(
            jax.ShapeDtypeStruct((ROWS, width), BF16),
            jax.ShapeDtypeStruct(dpre.shape, BF16),
            jax.ShapeDtypeStruct(gall.shape, BF16),
            jax.ShapeDtypeStruct(dxall.shape, BF16),
        ),
        in_specs=[pl.BlockSpec(memory_space=pltpu.SMEM)] + whole(18),
        out_specs=tuple(whole(4)),
        input_output_aliases={16: 1, 17: 2, 18: 3},
        scratch_shapes=[pltpu.VMEM((ROWS, width), BF16)],
        compiler_params=pltpu.CompilerParams(vmem_limit_bytes=8 * MIB),
        name="step",
    )(sc, packed, near, far, win, wout, q, k, v, gate, n2, att, ds, xn, r1, r2, dpre, gall, dxall)


def weights_kernel(xnt_ref, yut_ref, dpre_ref, gall_ref, out_ref, buf, sem):
    width = gall_ref.shape[1]
    block = 512
    first = 4 * width // block
    count = 5 * width // block

    def send(i, slot):
        there = pl.ds(pl.multiple_of(i * block, block), block)
        return pltpu.make_async_copy(buf.at[slot], out_ref.at[:, there], sem.at[slot])

    def run(i, carry):
        slot = lax.rem(i, 2)

        @pl.when(i >= 2)
        def _():
            send(i - 2, slot).wait()

        @pl.when(i < first)
        def _():
            cols = pl.ds(pl.multiple_of(i * block, block), block)
            buf[slot] = dot_nn(xnt_ref[...], dpre_ref[:, cols]).astype(BF16)

        @pl.when(i >= first)
        def _():
            cols = pl.ds(pl.multiple_of((i - first) * block, block), block)
            buf[slot] = dot_nn(yut_ref[...], gall_ref[:, cols]).astype(BF16)

        send(i, slot).start()
        return carry

    lax.fori_loop(0, count, run, 0)
    send(count - 2, lax.rem(count - 2, 2)).wait()
    send(count - 1, lax.rem(count - 1, 2)).wait()


def join_kernel(*refs):
    out_ref = refs[-1]
    at = 0
    while at < out_ref.shape[0]:
        for ref in refs[:-1]:
            rows = min(ref.shape[0], out_ref.shape[0] - at)
            if rows > 0:
                out_ref[at : at + rows, :] = ref[:rows, :]
                at += rows


def join(parts, rows):
    return pl.pallas_call(
        join_kernel,
        out_shape=jax.ShapeDtypeStruct((rows, parts[0].shape[1]), BF16),
        in_specs=whole(len(parts)),
        out_specs=pl.BlockSpec(memory_space=VMEM),
        compiler_params=pltpu.CompilerParams(vmem_limit_bytes=4 * MIB),
        name="join",
    )(*parts)


def widen_kernel(sum_ref, win_ref, wout_ref):
    split = win_ref.shape[1]
    win_ref[...] = sum_ref[:, :split].astype(F32)
    wout_ref[...] = sum_ref[:, split:].astype(F32)


def body(saved_inputs, cotangent, pack_lists, segment_ids, w_in, w_out):
    dp_count = lax.axis_size("dp")
    section_count = lax.axis_size("section")
    section_index = lax.axis_index("section")
    tok_rows, width = cotangent.shape
    micro_count, mb_rows = segment_ids.shape
    share = tok_rows // dp_count
    dp_index = lax.axis_index("dp")
    hops = section_count - 1
    half = dp_count // 2
    even = jnp.where(section_index % 2 == 0, half, 0)
    turned = pack_lists[0].reshape(dp_count, share)[::-1]
    turned = jnp.concatenate([turned, turned], axis=0)
    start = (dp_count - 1 - dp_index + even) % dp_count
    wanted = lax.dynamic_slice(turned, (start, 0), (half, share))
    picked = cotangent[wanted.reshape(-1)]
    tiled = jnp.tile(segment_ids, (1, GROUP))
    pos = jnp.arange(mb_rows)
    allowed = (segment_ids[:, :, None] == tiled[:, None, :]) & (
        (jnp.arange(WIDE) % mb_rows)[None, None, :] <= pos[None, :, None]
    )
    mask = allowed.astype(F32).reshape(tok_rows, WIDE)
    lag = lambda h: SKEW_NEAR * ((h + 1) // 2) + SKEW_FAR * (h // 2)
    chunks = tok_rows // ROWS
    steps = chunks + lag(hops)
    slots = jnp.arange(steps, dtype=jnp.int32) - lag(hops - section_index).astype(jnp.int32)
    valid = ((slots >= 0) & (slots < chunks)).astype(jnp.int32)
    first = section_index == hops
    source = jnp.where(first, 0, jnp.where(section_index % 2 == 0, 1, 2)).astype(jnp.int32)
    table = jnp.stack(
        [
            jnp.clip(slots, 0, chunks - 1),
            valid,
            jnp.broadcast_to(source, slots.shape),
            (jnp.clip(slots, 0, chunks - 1) * ROWS - dp_index * share) % tok_rows,
        ],
        axis=1,
    )
    scalars = [table[t] for t in range(steps)]
    picked, mask, scalars, saved_inputs, w_in, w_out = lax.optimization_barrier(
        (picked, mask, scalars, saved_inputs, w_in, w_out)
    )
    blocks = [picked[i * share : (i + 1) * share] for i in range(half)]
    blocks, w_in, w_out = lax.optimization_barrier((blocks, w_in, w_out))
    win, wout = turn_weights(w_in[0], w_out[0])
    parts = []
    for i in range(half):
        if i == half // 2:
            parts, win, blocks = lax.optimization_barrier((parts, win, blocks))
        pairs = []
        for rank in range(dp_count):
            pairs.append(((rank + i) % dp_count * section_count + hops, rank * section_count + hops))
            pairs.append(((rank + half + i) % dp_count * section_count + hops - 1, rank * section_count + hops - 1))
        parts.append(lax.ppermute(blocks[i], ("dp", "section"), pairs))
    q, k, v, gate, n2, att, ds, dpre, xn, xnt, yut, r1, r2 = forward(saved_inputs[0], mask, w_in[0])
    parts, q = lax.optimization_barrier((parts, q))
    saved = (q, k, v, gate, n2, att, ds, xn, r1, r2)
    mine = join(parts, tok_rows // 2)
    other = lax.ppermute(mine, "section", [(hops - 1, hops)])
    packed = join([mine, other], tok_rows + ROWS)

    near_perm = [(s, s - 1) for s in range(1, section_count, 2)]
    far_perm = [(s, s - 1) for s in range(2, section_count, 2)]

    zero = jnp.zeros((ROWS, width), BF16)
    nears, fars = {}, {}
    keep = lambda a: pltpu.with_memory_space_constraint(a, VMEM)
    dpre = keep(dpre)
    gall = keep(jnp.zeros((tok_rows, width), BF16))
    dxall = keep(jnp.zeros((tok_rows, width), BF16))
    for t in range(steps):
        near = nears.pop(t - SKEW_NEAR, zero)
        far = fars.pop(t - SKEW_FAR, zero)
        dx, dpre, gall, dxall = step(scalars[t], packed, near, far, win, wout, saved, dpre, gall, dxall)
        if t + SKEW_NEAR < steps:
            nears[t] = lax.ppermute(dx, "section", near_perm)
        if lag(1) <= t < chunks + lag(hops - 2):
            fars[t] = lax.ppermute(dx, "section", far_perm)

    store = pl.pallas_call(
        weights_kernel,
        out_shape=jax.ShapeDtypeStruct((width, 5 * width), BF16),
        in_specs=whole(4),
        out_specs=pl.BlockSpec(memory_space=pl.ANY),
        scratch_shapes=[pltpu.VMEM((2, width, 512), BF16), pltpu.SemaphoreType.DMA((2,))],
        compiler_params=pltpu.CompilerParams(vmem_limit_bytes=36 * MIB),
        name="weights",
    )(xnt, yut, dpre, gall)
    summed = lax.psum_scatter(store, "dp", scatter_dimension=0, tiled=True)
    rows = summed.shape[0]
    grad_in, grad_out = pl.pallas_call(
        widen_kernel,
        out_shape=(
            jax.ShapeDtypeStruct((rows, 4 * width), F32),
            jax.ShapeDtypeStruct((rows, width), F32),
        ),
        in_specs=whole(1),
        out_specs=tuple(whole(2)),
        name="widen",
    )(summed)
    return (dxall[None], grad_in[None], grad_out[None])


def solution(mesh):
    return jax.shard_map(
        body,
        mesh=mesh,
        in_specs=(
            P("section", "dp", None),
            P("dp", None),
            P("dp", None),
            P("dp", None),
            P("section", None, None),
            P("section", None, None),
        ),
        out_specs=(P("section", "dp", None), P("section", "dp", None), P("section", "dp", None)),
        check_vma=False,
    )
```

```python
import jax
import jax.numpy as jnp
from jax import lax
from jax.experimental import pallas as pl
from jax.experimental.pallas import tpu as pltpu
from jax.sharding import PartitionSpec as P

H = 16
HEAD = 64
MB = 64
WIDE = 256
GROUP = WIDE // HEAD
EPS = 1e-05
SKEW_NEAR = 1
SKEW_FAR = 2
ROWS = 2 * MB
MIB = 1 << 20
VMEM = pltpu.VMEM
F32 = jnp.float32
BF16 = jnp.bfloat16


def whole(count):
    return [pl.BlockSpec(memory_space=VMEM)] * count


def dot_nn(left, right):
    return lax.dot_general(left, right, (((1,), (0,)), ((), ())), preferred_element_type=F32)


def dot_nt(left, right):
    return lax.dot_general(left, right, (((1,), (1,)), ((), ())), preferred_element_type=F32)


def dot_tn(left, right):
    return lax.dot_general(left, right, (((0,), (0,)), ((), ())), preferred_element_type=F32)


def head_masks():
    lane = lax.broadcasted_iota(jnp.int32, (MB, WIDE), 1)
    return [((lane >= h * HEAD) & (lane < (h + 1) * HEAD)) for h in range(GROUP)]


def spread(block, masks):
    wide = block.astype(F32)
    return jnp.concatenate([jnp.where(m, wide, 0.0).astype(BF16) for m in masks], axis=0)


def gather_heads(full, masks):
    total = jnp.where(masks[0], full[:MB], 0.0)
    for h in range(1, GROUP):
        total = jnp.where(masks[h], full[h * MB : (h + 1) * MB], total)
    return total


def mean_rows(values):
    return jnp.sum(values, axis=-1, keepdims=True) * (1.0 / values.shape[-1])


def forward_kernel(
    x_ref, mask_ref, win_ref,
    q_ref, k_ref, v_ref, gate_ref, n2_ref, att_ref, ds_ref, dsil_ref, xn_ref, r1_ref, r2_ref, mixed,
):
    rows, width = x_ref.shape
    masks = head_masks()
    x = x_ref[...].astype(F32)
    centered = x - mean_rows(x)
    r1 = lax.rsqrt(mean_rows(centered * centered) + EPS)
    xn_ref[...] = (centered * r1).astype(BF16)
    r1_ref[...] = jnp.broadcast_to(r1, r1_ref.shape)
    outs = (gate_ref, v_ref, q_ref, k_ref)
    for cb in range(width // WIDE):
        cols = slice(cb * WIDE, (cb + 1) * WIDE)
        for part in range(4):
            wide = slice(part * width + cb * WIDE, part * width + (cb + 1) * WIDE)
            pre = dot_nn(xn_ref[...], win_ref[:, wide])
            sig = jax.nn.sigmoid(pre)
            act = pre * sig
            outs[part][:, cols] = act.astype(BF16)
            dsil_ref[:, wide] = (sig + act * (1.0 - sig)).astype(BF16)
        for m in range(rows // MB):
            rr = slice(m * MB, (m + 1) * MB)
            k4 = spread(k_ref[rr, cols], masks)
            v4 = spread(v_ref[rr, cols], masks)
            s = dot_nt(q_ref[rr, cols], k4) * (1.0 / 8.0)
            mask = mask_ref[rr, :]
            sg = jax.nn.sigmoid(s)
            sil = s * sg
            att = (sil * mask * (1.0 / MB)).astype(BF16)
            att_ref[rr, cols] = att
            ds_ref[rr, cols] = ((sg + sil * (1.0 - sg)) * mask * (1.0 / (8 * MB))).astype(BF16)
            mixed[rr, cols] = dot_nn(att, v4)
    mx = mixed[...]
    cm = mx - mean_rows(mx)
    r2 = lax.rsqrt(mean_rows(cm * cm) + EPS)
    r2_ref[...] = jnp.broadcast_to(r2, r2_ref.shape)
    n2_ref[...] = (cm * r2).astype(BF16)


def transpose_kernel(xn_ref, n2_ref, gate_ref, xnt_ref, yut_ref):
    xnt_ref[...] = xn_ref[...].T
    yu = n2_ref[...].astype(F32) * gate_ref[...].astype(F32)
    yut_ref[...] = yu.astype(BF16).T


def forward(x, mask, win):
    rows, width = x.shape
    block = 4 * MB
    small = jax.ShapeDtypeStruct((rows, width), BF16)
    big = jax.ShapeDtypeStruct((rows, 4 * width), BF16)
    stat = jax.ShapeDtypeStruct((rows, 128), F32)
    shapes = (small,) * 7 + (big, small, stat, stat)
    lines = lambda a: pl.BlockSpec((block, a.shape[1]), lambda i: (i, 0))
    return pl.pallas_call(
        forward_kernel,
        out_shape=shapes,
        grid=(rows // block,),
        in_specs=[
            lines(x),
            lines(mask),
            pl.BlockSpec(win.shape, lambda i: (0, 0), pipeline_mode=pl.Buffered(1)),
        ],
        out_specs=tuple(lines(a) for a in shapes),
        scratch_shapes=[pltpu.VMEM((block, width), F32)],
        compiler_params=pltpu.CompilerParams(vmem_limit_bytes=58 * MIB),
        name="forward",
    )(x, mask, win)


def turn(xn, n2, gate):
    turned = jax.ShapeDtypeStruct(xn.shape[::-1], BF16)
    return pl.pallas_call(
        transpose_kernel,
        out_shape=(turned, turned),
        in_specs=whole(3),
        out_specs=tuple(whole(2)),
        compiler_params=pltpu.CompilerParams(vmem_limit_bytes=8 * MIB),
        name="turn",
    )(xn, n2, gate)


def step_kernel(
    sc_ref, packed_ref, near_ref, far_ref, win_ref, wout_ref, q_ref, k_ref, v_ref, gate_ref, n2_ref, att_ref,
    ds_ref, xn_ref, r1_ref, r2_ref, dpre_in, gall_in, dxall_in,
    out_ref, dpre_ref, gall_ref, dxall_ref, gbuf,
):
    slot, valid, source = sc_ref[0], sc_ref[1], sc_ref[2]
    width = out_ref.shape[1]

    @pl.when(valid == 1)
    def _():
        rr = pl.ds(pl.multiple_of(slot * ROWS, ROWS), ROWS)

        @pl.when(source == 0)
        def _():
            gbuf[...] = packed_ref[rr, :]

        @pl.when(source == 1)
        def _():
            gbuf[...] = near_ref[...]

        @pl.when(source == 2)
        def _():
            gbuf[...] = far_ref[...]

        masks = head_masks()
        g = gbuf[...]
        gall_ref[rr, :] = g
        d_yu = dot_nn(g, wout_ref[...]).astype(BF16).astype(F32)
        n2 = n2_ref[rr, :].astype(F32)
        gate = gate_ref[rr, :].astype(F32)
        d_gate = d_yu * n2
        d_n2 = d_yu * gate
        r2 = r2_ref[rr, :][:, :1]
        d_mixed = (r2 * (d_n2 - mean_rows(d_n2) - n2 * mean_rows(d_n2 * n2))).astype(BF16)
        dpre_ref[rr, :width] = (d_gate * dpre_in[rr, :width].astype(F32)).astype(BF16)
        for c in range(width // WIDE):
            lo = c * WIDE
            cols = slice(lo, lo + WIDE)
            for m in range(ROWS // MB):
                mm = pl.ds(pl.multiple_of(slot * ROWS + m * MB, MB), MB)
                do4 = d_mixed[m * MB : (m + 1) * MB, cols]
                q4 = q_ref[mm, cols]
                k4 = spread(k_ref[mm, cols], masks)
                v4 = spread(v_ref[mm, cols], masks)
                att = att_ref[mm, cols]
                d_att = dot_nt(do4, v4)
                d_s = (d_att * ds_ref[mm, cols].astype(F32)).astype(BF16)
                d_q = dot_nn(d_s, k4)
                d_k = gather_heads(dot_tn(d_s, q4), masks)
                d_v = gather_heads(dot_tn(att, do4), masks)
                for part, val in ((1, d_v), (2, d_q), (3, d_k)):
                    at = slice(part * width + lo, part * width + lo + WIDE)
                    dpre_ref[mm, at] = (val * dpre_in[mm, at].astype(F32)).astype(BF16)
        d_xn = dot_nn(dpre_ref[rr, :], win_ref[...])
        xn = xn_ref[rr, :].astype(F32)
        r1 = r1_ref[rr, :][:, :1]
        dx = g.astype(F32) + r1 * (d_xn - mean_rows(d_xn) - xn * mean_rows(d_xn * xn))
        dx = dx.astype(BF16)
        out_ref[...] = dx
        dxall_ref[rr, :] = dx


def turn_weights_kernel(win_ref, wout_ref, wint_ref, woutt_ref):
    wint_ref[...] = win_ref[...].T
    woutt_ref[...] = wout_ref[...].T


def turn_weights(win, wout):
    shapes = [jax.ShapeDtypeStruct(w.shape[::-1], BF16) for w in (win, wout)]
    return pl.pallas_call(
        turn_weights_kernel,
        out_shape=tuple(shapes),
        in_specs=whole(2),
        out_specs=tuple(whole(2)),
        compiler_params=pltpu.CompilerParams(vmem_limit_bytes=4 * MIB),
        name="turn_weights",
    )(win, wout)


def step(sc, packed, near, far, win, wout, saved, dpre, gall, dxall):
    q, k, v, gate, n2, att, ds, xn, r1, r2 = saved
    width = q.shape[1]
    return pl.pallas_call(
        step_kernel,
        out_shape=(
            jax.ShapeDtypeStruct((ROWS, width), BF16),
            jax.ShapeDtypeStruct(dpre.shape, BF16),
            jax.ShapeDtypeStruct(gall.shape, BF16),
            jax.ShapeDtypeStruct(dxall.shape, BF16),
        ),
        in_specs=[pl.BlockSpec(memory_space=pltpu.SMEM)] + whole(18),
        out_specs=tuple(whole(4)),
        input_output_aliases={16: 1, 17: 2, 18: 3},
        scratch_shapes=[pltpu.VMEM((ROWS, width), BF16)],
        compiler_params=pltpu.CompilerParams(vmem_limit_bytes=8 * MIB),
        name="step",
    )(sc, packed, near, far, win, wout, q, k, v, gate, n2, att, ds, xn, r1, r2, dpre, gall, dxall)


def weights_kernel(xnt_ref, yut_ref, dpre_ref, gall_ref, out_ref, buf, sem):
    width = gall_ref.shape[1]
    block = 512
    first = 4 * width // block
    count = 5 * width // block

    def send(i, slot):
        there = pl.ds(pl.multiple_of(i * block, block), block)
        return pltpu.make_async_copy(buf.at[slot], out_ref.at[:, there], sem.at[slot])

    def run(i, carry):
        slot = lax.rem(i, 2)

        @pl.when(i >= 2)
        def _():
            send(i - 2, slot).wait()

        @pl.when(i < first)
        def _():
            cols = pl.ds(pl.multiple_of(i * block, block), block)
            buf[slot] = dot_nn(xnt_ref[...], dpre_ref[:, cols]).astype(BF16)

        @pl.when(i >= first)
        def _():
            cols = pl.ds(pl.multiple_of((i - first) * block, block), block)
            buf[slot] = dot_nn(yut_ref[...], gall_ref[:, cols]).astype(BF16)

        send(i, slot).start()
        return carry

    lax.fori_loop(0, count, run, 0)
    send(count - 2, lax.rem(count - 2, 2)).wait()
    send(count - 1, lax.rem(count - 1, 2)).wait()


def widen_kernel(sum_ref, win_ref, wout_ref):
    split = win_ref.shape[1]
    win_ref[...] = sum_ref[:, :split].astype(F32)
    wout_ref[...] = sum_ref[:, split:].astype(F32)


def body(saved_inputs, cotangent, pack_lists, segment_ids, w_in, w_out):
    dp_count = lax.axis_size("dp")
    section_count = lax.axis_size("section")
    section_index = lax.axis_index("section")
    tok_rows, width = cotangent.shape
    micro_count, mb_rows = segment_ids.shape
    share = tok_rows // dp_count
    hops = section_count - 1
    picked = cotangent[pack_lists[0]]
    tiled = jnp.tile(segment_ids, (1, GROUP))
    pos = jnp.arange(mb_rows)
    allowed = (segment_ids[:, :, None] == tiled[:, None, :]) & (
        (jnp.arange(WIDE) % mb_rows)[None, None, :] <= pos[None, :, None]
    )
    mask = allowed.astype(F32).reshape(tok_rows, WIDE)
    lag = lambda h: SKEW_NEAR * ((h + 1) // 2) + SKEW_FAR * (h // 2)
    chunks = tok_rows // ROWS
    steps = chunks + lag(hops)
    slots = jnp.arange(steps, dtype=jnp.int32) - lag(hops - section_index).astype(jnp.int32)
    valid = ((slots >= 0) & (slots < chunks)).astype(jnp.int32)
    first = section_index == hops
    source = jnp.where(first, 0, jnp.where(section_index % 2 == 0, 1, 2)).astype(jnp.int32)
    table = jnp.stack(
        [
            jnp.clip(slots, 0, chunks - 1),
            valid,
            jnp.broadcast_to(source, slots.shape),
        ],
        axis=1,
    )
    scalars = [table[t] for t in range(steps)]
    picked, mask, scalars, saved_inputs, w_in, w_out = lax.optimization_barrier(
        (picked, mask, scalars, saved_inputs, w_in, w_out)
    )
    packed = lax.all_to_all(
        picked.reshape(dp_count, share, width), "dp", split_axis=0, concat_axis=0, tiled=True
    ).reshape(tok_rows, width)
    made = forward(saved_inputs[0], mask, w_in[0])
    packed, made, w_in, w_out = lax.optimization_barrier((packed, made, w_in, w_out))
    win, wout = turn_weights(w_in[0], w_out[0])
    q, k, v, gate, n2, att, ds, dpre, xn, r1, r2 = made
    xnt, yut = turn(xn, n2, gate)
    saved = (q, k, v, gate, n2, att, ds, xn, r1, r2)

    near_perm = [(s, s - 1) for s in range(1, section_count, 2)]
    far_perm = [(s, s - 1) for s in range(2, section_count, 2)]

    zero = jnp.zeros((ROWS, width), BF16)
    nears, fars = {}, {}
    keep = lambda a: pltpu.with_memory_space_constraint(a, VMEM)
    dpre = keep(dpre)
    gall = keep(jnp.zeros((tok_rows, width), BF16))
    dxall = keep(jnp.zeros((tok_rows, width), BF16))
    for t in range(steps):
        near = nears.pop(t - SKEW_NEAR, zero)
        far = fars.pop(t - SKEW_FAR, zero)
        dx, dpre, gall, dxall = step(scalars[t], packed, near, far, win, wout, saved, dpre, gall, dxall)
        if t + SKEW_NEAR < steps:
            nears[t] = lax.ppermute(dx, "section", near_perm)
        if lag(1) <= t < chunks + lag(hops - 2):
            fars[t] = lax.ppermute(dx, "section", far_perm)

    store = pl.pallas_call(
        weights_kernel,
        out_shape=jax.ShapeDtypeStruct((width, 5 * width), BF16),
        in_specs=whole(4),
        out_specs=pl.BlockSpec(memory_space=pl.ANY),
        scratch_shapes=[pltpu.VMEM((2, width, 512), BF16), pltpu.SemaphoreType.DMA((2,))],
        compiler_params=pltpu.CompilerParams(vmem_limit_bytes=34 * MIB),
        name="weights",
    )(xnt, yut, dpre, gall)
    summed = lax.psum_scatter(store, "dp", scatter_dimension=0, tiled=True)
    rows = summed.shape[0]
    grad_in, grad_out = pl.pallas_call(
        widen_kernel,
        out_shape=(
            jax.ShapeDtypeStruct((rows, 4 * width), F32),
            jax.ShapeDtypeStruct((rows, width), F32),
        ),
        in_specs=whole(1),
        out_specs=tuple(whole(2)),
        name="widen",
    )(summed)
    return (dxall[None], grad_in[None], grad_out[None])


def solution(mesh):
    return jax.shard_map(
        body,
        mesh=mesh,
        in_specs=(
            P("section", "dp", None),
            P("dp", None),
            P("dp", None),
            P("dp", None),
            P("section", None, None),
            P("section", None, None),
        ),
        out_specs=(P("section", "dp", None), P("section", "dp", None), P("section", "dp", None)),
        check_vma=False,
    )
```

```python
import jax
import jax.numpy as jnp
from jax import lax
from jax.experimental import pallas as pl
from jax.experimental.pallas import tpu as pltpu
from jax.sharding import PartitionSpec as P

H = 16
HEAD = 64
MB = 64
WIDE = 256
GROUP = WIDE // HEAD
EPS = 1e-05
SKEW = 2
ROWS = 2 * MB
MIB = 1 << 20
VMEM = pltpu.VMEM
F32 = jnp.float32
BF16 = jnp.bfloat16


def whole(count):
    return [pl.BlockSpec(memory_space=VMEM)] * count


def dot_nn(left, right):
    return lax.dot_general(left, right, (((1,), (0,)), ((), ())), preferred_element_type=F32)


def dot_nt(left, right):
    return lax.dot_general(left, right, (((1,), (1,)), ((), ())), preferred_element_type=F32)


def dot_tn(left, right):
    return lax.dot_general(left, right, (((0,), (0,)), ((), ())), preferred_element_type=F32)


def head_masks():
    lane = lax.broadcasted_iota(jnp.int32, (MB, WIDE), 1)
    return [((lane >= h * HEAD) & (lane < (h + 1) * HEAD)) for h in range(GROUP)]


def spread(block, masks):
    wide = block.astype(F32)
    return jnp.concatenate([jnp.where(m, wide, 0.0).astype(BF16) for m in masks], axis=0)


def gather_heads(full, masks):
    total = jnp.where(masks[0], full[:MB], 0.0)
    for h in range(1, GROUP):
        total = jnp.where(masks[h], full[h * MB : (h + 1) * MB], total)
    return total


def mean_rows(values):
    return jnp.sum(values, axis=-1, keepdims=True) * (1.0 / values.shape[-1])


def forward_kernel(
    x_ref, mask_ref, win_ref,
    q_ref, k_ref, v_ref, gate_ref, n2_ref, att_ref, ds_ref, dsil_ref, xn_ref, r1_ref, r2_ref, mixed,
):
    rows, width = x_ref.shape
    masks = head_masks()
    x = x_ref[...].astype(F32)
    centered = x - mean_rows(x)
    r1 = lax.rsqrt(mean_rows(centered * centered) + EPS)
    xn_ref[...] = (centered * r1).astype(BF16)
    r1_ref[...] = jnp.broadcast_to(r1, r1_ref.shape)
    outs = (gate_ref, v_ref, q_ref, k_ref)
    for cb in range(width // WIDE):
        cols = slice(cb * WIDE, (cb + 1) * WIDE)
        for part in range(4):
            wide = slice(part * width + cb * WIDE, part * width + (cb + 1) * WIDE)
            pre = dot_nn(xn_ref[...], win_ref[:, wide])
            sig = jax.nn.sigmoid(pre)
            act = pre * sig
            outs[part][:, cols] = act.astype(BF16)
            dsil_ref[:, wide] = (sig + act * (1.0 - sig)).astype(BF16)
        for m in range(rows // MB):
            rr = slice(m * MB, (m + 1) * MB)
            k4 = spread(k_ref[rr, cols], masks)
            v4 = spread(v_ref[rr, cols], masks)
            s = dot_nt(q_ref[rr, cols], k4) * (1.0 / 8.0)
            mask = mask_ref[rr, :]
            sg = jax.nn.sigmoid(s)
            sil = s * sg
            att = (sil * mask * (1.0 / MB)).astype(BF16)
            att_ref[rr, cols] = att
            ds_ref[rr, cols] = ((sg + sil * (1.0 - sg)) * mask * (1.0 / (8 * MB))).astype(BF16)
            mixed[rr, cols] = dot_nn(att, v4)
    mx = mixed[...]
    cm = mx - mean_rows(mx)
    r2 = lax.rsqrt(mean_rows(cm * cm) + EPS)
    r2_ref[...] = jnp.broadcast_to(r2, r2_ref.shape)
    n2_ref[...] = (cm * r2).astype(BF16)


def transpose_kernel(xn_ref, n2_ref, gate_ref, xnt_ref, yut_ref):
    xnt_ref[...] = xn_ref[...].T
    yu = n2_ref[...].astype(F32) * gate_ref[...].astype(F32)
    yut_ref[...] = yu.astype(BF16).T


def forward(x, mask, win):
    rows, width = x.shape
    block = 4 * MB
    small = jax.ShapeDtypeStruct((rows, width), BF16)
    big = jax.ShapeDtypeStruct((rows, 4 * width), BF16)
    stat = jax.ShapeDtypeStruct((rows, 128), F32)
    shapes = (small,) * 7 + (big, small, stat, stat)
    lines = lambda a: pl.BlockSpec((block, a.shape[1]), lambda i: (i, 0))
    return pl.pallas_call(
        forward_kernel,
        out_shape=shapes,
        grid=(rows // block,),
        in_specs=[
            lines(x),
            lines(mask),
            pl.BlockSpec(win.shape, lambda i: (0, 0), pipeline_mode=pl.Buffered(1)),
        ],
        out_specs=tuple(lines(a) for a in shapes),
        scratch_shapes=[pltpu.VMEM((block, width), F32)],
        compiler_params=pltpu.CompilerParams(vmem_limit_bytes=58 * MIB),
        name="forward",
    )(x, mask, win)


def turn(xn, n2, gate):
    turned = jax.ShapeDtypeStruct(xn.shape[::-1], BF16)
    return pl.pallas_call(
        transpose_kernel,
        out_shape=(turned, turned),
        in_specs=whole(3),
        out_specs=tuple(whole(2)),
        compiler_params=pltpu.CompilerParams(vmem_limit_bytes=8 * MIB),
        name="turn",
    )(xn, n2, gate)


def step_kernel(
    sc_ref, packed_ref, got_ref, win_ref, wout_ref, q_ref, k_ref, v_ref, gate_ref, n2_ref, att_ref,
    ds_ref, xn_ref, r1_ref, r2_ref, dpre_in, gall_in, dxall_in,
    out_ref, dpre_ref, gall_ref, dxall_ref, gbuf,
):
    slot, valid, source = sc_ref[0], sc_ref[1], sc_ref[2]
    width = out_ref.shape[1]

    @pl.when(valid == 1)
    def _():
        rr = pl.ds(pl.multiple_of(slot * ROWS, ROWS), ROWS)

        @pl.when(source == 0)
        def _():
            gbuf[...] = packed_ref[rr, :]

        @pl.when(source == 1)
        def _():
            gbuf[...] = got_ref[...]

        masks = head_masks()
        g = gbuf[...]
        gall_ref[rr, :] = g
        d_yu = dot_nn(g, wout_ref[...]).astype(BF16).astype(F32)
        n2 = n2_ref[rr, :].astype(F32)
        gate = gate_ref[rr, :].astype(F32)
        d_gate = d_yu * n2
        d_n2 = d_yu * gate
        r2 = r2_ref[rr, :][:, :1]
        d_mixed = (r2 * (d_n2 - mean_rows(d_n2) - n2 * mean_rows(d_n2 * n2))).astype(BF16)
        dpre_ref[rr, :width] = (d_gate * dpre_in[rr, :width].astype(F32)).astype(BF16)
        for c in range(width // WIDE):
            lo = c * WIDE
            cols = slice(lo, lo + WIDE)
            for m in range(ROWS // MB):
                mm = pl.ds(pl.multiple_of(slot * ROWS + m * MB, MB), MB)
                do4 = d_mixed[m * MB : (m + 1) * MB, cols]
                q4 = q_ref[mm, cols]
                k4 = spread(k_ref[mm, cols], masks)
                v4 = spread(v_ref[mm, cols], masks)
                att = att_ref[mm, cols]
                d_att = dot_nt(do4, v4)
                d_s = (d_att * ds_ref[mm, cols].astype(F32)).astype(BF16)
                d_q = dot_nn(d_s, k4)
                d_k = gather_heads(dot_tn(d_s, q4), masks)
                d_v = gather_heads(dot_tn(att, do4), masks)
                for part, val in ((1, d_v), (2, d_q), (3, d_k)):
                    at = slice(part * width + lo, part * width + lo + WIDE)
                    dpre_ref[mm, at] = (val * dpre_in[mm, at].astype(F32)).astype(BF16)
        d_xn = dot_nn(dpre_ref[rr, :], win_ref[...])
        xn = xn_ref[rr, :].astype(F32)
        r1 = r1_ref[rr, :][:, :1]
        dx = g.astype(F32) + r1 * (d_xn - mean_rows(d_xn) - xn * mean_rows(d_xn * xn))
        dx = dx.astype(BF16)
        out_ref[...] = dx
        dxall_ref[rr, :] = dx


def turn_weights_kernel(win_ref, wout_ref, wint_ref, woutt_ref):
    wint_ref[...] = win_ref[...].T
    woutt_ref[...] = wout_ref[...].T


def turn_weights(win, wout):
    shapes = [jax.ShapeDtypeStruct(w.shape[::-1], BF16) for w in (win, wout)]
    return pl.pallas_call(
        turn_weights_kernel,
        out_shape=tuple(shapes),
        in_specs=whole(2),
        out_specs=tuple(whole(2)),
        compiler_params=pltpu.CompilerParams(vmem_limit_bytes=4 * MIB),
        name="turn_weights",
    )(win, wout)


def step(sc, packed, got, win, wout, saved, dpre, gall, dxall):
    q, k, v, gate, n2, att, ds, xn, r1, r2 = saved
    width = q.shape[1]
    return pl.pallas_call(
        step_kernel,
        out_shape=(
            jax.ShapeDtypeStruct((ROWS, width), BF16),
            jax.ShapeDtypeStruct(dpre.shape, BF16),
            jax.ShapeDtypeStruct(gall.shape, BF16),
            jax.ShapeDtypeStruct(dxall.shape, BF16),
        ),
        in_specs=[pl.BlockSpec(memory_space=pltpu.SMEM)] + whole(17),
        out_specs=tuple(whole(4)),
        input_output_aliases={15: 1, 16: 2, 17: 3},
        scratch_shapes=[pltpu.VMEM((ROWS, width), BF16)],
        compiler_params=pltpu.CompilerParams(vmem_limit_bytes=8 * MIB),
        name="step",
    )(sc, packed, got, win, wout, q, k, v, gate, n2, att, ds, xn, r1, r2, dpre, gall, dxall)


def weights_kernel(xnt_ref, yut_ref, dpre_ref, gall_ref, out_ref, buf, sem):
    width = gall_ref.shape[1]
    block = 512
    first = 4 * width // block
    count = 5 * width // block

    def send(i, slot):
        there = pl.ds(pl.multiple_of(i * block, block), block)
        return pltpu.make_async_copy(buf.at[slot], out_ref.at[:, there], sem.at[slot])

    def run(i, carry):
        slot = lax.rem(i, 2)

        @pl.when(i >= 2)
        def _():
            send(i - 2, slot).wait()

        @pl.when(i < first)
        def _():
            cols = pl.ds(pl.multiple_of(i * block, block), block)
            buf[slot] = dot_nn(xnt_ref[...], dpre_ref[:, cols]).astype(BF16)

        @pl.when(i >= first)
        def _():
            cols = pl.ds(pl.multiple_of((i - first) * block, block), block)
            buf[slot] = dot_nn(yut_ref[...], gall_ref[:, cols]).astype(BF16)

        send(i, slot).start()
        return carry

    lax.fori_loop(0, count, run, 0)
    send(count - 2, lax.rem(count - 2, 2)).wait()
    send(count - 1, lax.rem(count - 1, 2)).wait()


def widen_kernel(sum_ref, win_ref, wout_ref):
    split = win_ref.shape[1]
    win_ref[...] = sum_ref[:, :split].astype(F32)
    wout_ref[...] = sum_ref[:, split:].astype(F32)


def body(saved_inputs, cotangent, pack_lists, segment_ids, w_in, w_out):
    dp_count = lax.axis_size("dp")
    section_count = lax.axis_size("section")
    section_index = lax.axis_index("section")
    tok_rows, width = cotangent.shape
    micro_count, mb_rows = segment_ids.shape
    share = tok_rows // dp_count
    hops = section_count - 1
    picked = cotangent[pack_lists[0]]
    tiled = jnp.tile(segment_ids, (1, GROUP))
    pos = jnp.arange(mb_rows)
    allowed = (segment_ids[:, :, None] == tiled[:, None, :]) & (
        (jnp.arange(WIDE) % mb_rows)[None, None, :] <= pos[None, :, None]
    )
    mask = allowed.astype(F32).reshape(tok_rows, WIDE)
    lag = lambda h: SKEW * h
    chunks = tok_rows // ROWS
    steps = chunks + lag(hops)
    slots = jnp.arange(steps, dtype=jnp.int32) - lag(hops - section_index)
    valid = ((slots >= 0) & (slots < chunks)).astype(jnp.int32)
    first = section_index == hops
    source = jnp.where(first, 0, 1).astype(jnp.int32)
    table = jnp.stack(
        [
            jnp.clip(slots, 0, chunks - 1),
            valid,
            jnp.broadcast_to(source, slots.shape),
        ],
        axis=1,
    )
    scalars = [table[t] for t in range(steps)]
    picked, mask, scalars, saved_inputs, w_in, w_out = lax.optimization_barrier(
        (picked, mask, scalars, saved_inputs, w_in, w_out)
    )
    packed = lax.all_to_all(
        picked.reshape(dp_count, share, width), "dp", split_axis=0, concat_axis=0, tiled=True
    ).reshape(tok_rows, width)
    made = forward(saved_inputs[0], mask, w_in[0])
    packed, made, w_in, w_out = lax.optimization_barrier((packed, made, w_in, w_out))
    win, wout = turn_weights(w_in[0], w_out[0])
    q, k, v, gate, n2, att, ds, dpre, xn, r1, r2 = made
    xnt, yut = turn(xn, n2, gate)
    saved = (q, k, v, gate, n2, att, ds, xn, r1, r2)

    down = [(s, s - 1) for s in range(1, section_count)]

    zero = jnp.zeros((ROWS, width), BF16)
    moving = {}
    keep = lambda a: pltpu.with_memory_space_constraint(a, VMEM)
    dpre = keep(dpre)
    gall = keep(jnp.zeros((tok_rows, width), BF16))
    dxall = keep(jnp.zeros((tok_rows, width), BF16))
    for t in range(steps):
        got = moving.pop(t - SKEW, zero)
        dx, dpre, gall, dxall = step(scalars[t], packed, got, win, wout, saved, dpre, gall, dxall)
        if t + SKEW < steps:
            moving[t] = lax.ppermute(dx, "section", down)

    store = pl.pallas_call(
        weights_kernel,
        out_shape=jax.ShapeDtypeStruct((width, 5 * width), BF16),
        in_specs=whole(4),
        out_specs=pl.BlockSpec(memory_space=pl.ANY),
        scratch_shapes=[pltpu.VMEM((2, width, 512), BF16), pltpu.SemaphoreType.DMA((2,))],
        compiler_params=pltpu.CompilerParams(vmem_limit_bytes=34 * MIB),
        name="weights",
    )(xnt, yut, dpre, gall)
    summed = lax.psum_scatter(store, "dp", scatter_dimension=0, tiled=True)
    rows = summed.shape[0]
    grad_in, grad_out = pl.pallas_call(
        widen_kernel,
        out_shape=(
            jax.ShapeDtypeStruct((rows, 4 * width), F32),
            jax.ShapeDtypeStruct((rows, width), F32),
        ),
        in_specs=whole(1),
        out_specs=tuple(whole(2)),
        name="widen",
    )(summed)
    return (dxall[None], grad_in[None], grad_out[None])


def solution(mesh):
    return jax.shard_map(
        body,
        mesh=mesh,
        in_specs=(
            P("section", "dp", None),
            P("dp", None),
            P("dp", None),
            P("dp", None),
            P("section", None, None),
            P("section", None, None),
        ),
        out_specs=(P("section", "dp", None), P("section", "dp", None), P("section", "dp", None)),
        check_vma=False,
    )
```

```python
import jax
import jax.numpy as jnp
from jax import lax
from jax.experimental import pallas as pl
from jax.experimental.pallas import tpu as pltpu
from jax.sharding import PartitionSpec as P

H = 16
HEAD = 64
MB = 64
WIDE = 256
GROUP = WIDE // HEAD
EPS = 1e-05
SKEW = 2
ROWS = 2 * MB
MIB = 1 << 20
VMEM = pltpu.VMEM
F32 = jnp.float32
BF16 = jnp.bfloat16


def whole(count):
    return [pl.BlockSpec(memory_space=VMEM)] * count


def dot_nn(left, right):
    return lax.dot_general(left, right, (((1,), (0,)), ((), ())), preferred_element_type=F32)


def dot_nt(left, right):
    return lax.dot_general(left, right, (((1,), (1,)), ((), ())), preferred_element_type=F32)


def dot_tn(left, right):
    return lax.dot_general(left, right, (((0,), (0,)), ((), ())), preferred_element_type=F32)


def head_masks():
    lane = lax.broadcasted_iota(jnp.int32, (MB, WIDE), 1)
    return [((lane >= h * HEAD) & (lane < (h + 1) * HEAD)) for h in range(GROUP)]


def spread(block, masks):
    wide = block.astype(F32)
    return jnp.concatenate([jnp.where(m, wide, 0.0).astype(BF16) for m in masks], axis=0)


def gather_heads(full, masks):
    total = jnp.where(masks[0], full[:MB], 0.0)
    for h in range(1, GROUP):
        total = jnp.where(masks[h], full[h * MB : (h + 1) * MB], total)
    return total


def mean_rows(values):
    return jnp.sum(values, axis=-1, keepdims=True) * (1.0 / values.shape[-1])


def forward_kernel(
    x_ref, mask_ref, win_ref,
    q_ref, k_ref, v_ref, gate_ref, n2_ref, att_ref, ds_ref, dsil_ref, xn_ref, r1_ref, r2_ref, mixed,
):
    rows, width = x_ref.shape
    masks = head_masks()
    x = x_ref[...].astype(F32)
    centered = x - mean_rows(x)
    r1 = lax.rsqrt(mean_rows(centered * centered) + EPS)
    xn_ref[...] = (centered * r1).astype(BF16)
    r1_ref[...] = jnp.broadcast_to(r1, r1_ref.shape)
    outs = (gate_ref, v_ref, q_ref, k_ref)
    for cb in range(width // WIDE):
        cols = slice(cb * WIDE, (cb + 1) * WIDE)
        for part in range(4):
            wide = slice(part * width + cb * WIDE, part * width + (cb + 1) * WIDE)
            pre = dot_nn(xn_ref[...], win_ref[:, wide])
            sig = jax.nn.sigmoid(pre)
            act = pre * sig
            outs[part][:, cols] = act.astype(BF16)
            dsil_ref[:, wide] = (sig + act * (1.0 - sig)).astype(BF16)
        for m in range(rows // MB):
            rr = slice(m * MB, (m + 1) * MB)
            k4 = spread(k_ref[rr, cols], masks)
            v4 = spread(v_ref[rr, cols], masks)
            s = dot_nt(q_ref[rr, cols], k4) * (1.0 / 8.0)
            mask = mask_ref[rr, :]
            sg = jax.nn.sigmoid(s)
            sil = s * sg
            att = (sil * mask * (1.0 / MB)).astype(BF16)
            att_ref[rr, cols] = att
            ds_ref[rr, cols] = ((sg + sil * (1.0 - sg)) * mask * (1.0 / (8 * MB))).astype(BF16)
            mixed[rr, cols] = dot_nn(att, v4)
    mx = mixed[...]
    cm = mx - mean_rows(mx)
    r2 = lax.rsqrt(mean_rows(cm * cm) + EPS)
    r2_ref[...] = jnp.broadcast_to(r2, r2_ref.shape)
    n2_ref[...] = (cm * r2).astype(BF16)


def transpose_kernel(xn_ref, n2_ref, gate_ref, xnt_ref, yut_ref):
    xnt_ref[...] = xn_ref[...].T
    yu = n2_ref[...].astype(F32) * gate_ref[...].astype(F32)
    yut_ref[...] = yu.astype(BF16).T


def forward(x, mask, win):
    rows, width = x.shape
    block = 4 * MB
    small = jax.ShapeDtypeStruct((rows, width), BF16)
    big = jax.ShapeDtypeStruct((rows, 4 * width), BF16)
    stat = jax.ShapeDtypeStruct((rows, 128), F32)
    shapes = (small,) * 7 + (big, small, stat, stat)
    lines = lambda a: pl.BlockSpec((block, a.shape[1]), lambda i: (i, 0))
    return pl.pallas_call(
        forward_kernel,
        out_shape=shapes,
        grid=(rows // block,),
        in_specs=[
            lines(x),
            lines(mask),
            pl.BlockSpec(win.shape, lambda i: (0, 0), pipeline_mode=pl.Buffered(1)),
        ],
        out_specs=tuple(lines(a) for a in shapes),
        scratch_shapes=[pltpu.VMEM((block, width), F32)],
        compiler_params=pltpu.CompilerParams(vmem_limit_bytes=58 * MIB),
        name="forward",
    )(x, mask, win)


def turn(xn, n2, gate):
    turned = jax.ShapeDtypeStruct(xn.shape[::-1], BF16)
    return pl.pallas_call(
        transpose_kernel,
        out_shape=(turned, turned),
        in_specs=whole(3),
        out_specs=tuple(whole(2)),
        compiler_params=pltpu.CompilerParams(vmem_limit_bytes=8 * MIB),
        name="turn",
    )(xn, n2, gate)


def step_kernel(
    sc_ref, packed_ref, got_ref, win_ref, wout_ref, q_ref, k_ref, v_ref, gate_ref, n2_ref, att_ref,
    ds_ref, xn_ref, r1_ref, r2_ref, dpre_in, gall_in, dxall_in,
    out_ref, dpre_ref, gall_ref, dxall_ref, gbuf, mixed_ref,
):
    slot, valid, source = sc_ref[0], sc_ref[1], sc_ref[2]
    width = out_ref.shape[1]

    @pl.when(valid == 1)
    def _():
        rr = pl.ds(pl.multiple_of(slot * ROWS, ROWS), ROWS)

        @pl.when(source == 0)
        def _():
            gbuf[...] = packed_ref[rr, :]

        @pl.when(source == 1)
        def _():
            gbuf[...] = got_ref[...]

        masks = head_masks()
        g = gbuf[...]
        gall_ref[rr, :] = g
        d_yu = dot_nn(g, wout_ref[...]).astype(BF16).astype(F32)
        n2 = n2_ref[rr, :].astype(F32)
        gate = gate_ref[rr, :].astype(F32)
        d_gate = d_yu * n2
        d_n2 = d_yu * gate
        r2 = r2_ref[rr, :][:, :1]
        d_mixed = (r2 * (d_n2 - mean_rows(d_n2) - n2 * mean_rows(d_n2 * n2))).astype(BF16)
        dpre_ref[rr, :width] = (d_gate * dpre_in[rr, :width].astype(F32)).astype(BF16)
        mixed_ref[...] = d_mixed

        def attention(m, carry):
            here = pl.ds(pl.multiple_of(m * MB, MB), MB)
            mm = pl.ds(pl.multiple_of(slot * ROWS + m * MB, MB), MB)
            for c in range(width // WIDE):
                lo = c * WIDE
                cols = slice(lo, lo + WIDE)
                do4 = mixed_ref[here, cols]
                q4 = q_ref[mm, cols]
                k4 = spread(k_ref[mm, cols], masks)
                v4 = spread(v_ref[mm, cols], masks)
                att = att_ref[mm, cols]
                d_att = dot_nt(do4, v4)
                d_s = (d_att * ds_ref[mm, cols].astype(F32)).astype(BF16)
                d_q = dot_nn(d_s, k4)
                d_k = gather_heads(dot_tn(d_s, q4), masks)
                d_v = gather_heads(dot_tn(att, do4), masks)
                for part, val in ((1, d_v), (2, d_q), (3, d_k)):
                    at = slice(part * width + lo, part * width + lo + WIDE)
                    dpre_ref[mm, at] = (val * dpre_in[mm, at].astype(F32)).astype(BF16)
            return carry

        lax.fori_loop(0, ROWS // MB, attention, 0)
        d_xn = dot_nn(dpre_ref[rr, :], win_ref[...])
        xn = xn_ref[rr, :].astype(F32)
        r1 = r1_ref[rr, :][:, :1]
        dx = g.astype(F32) + r1 * (d_xn - mean_rows(d_xn) - xn * mean_rows(d_xn * xn))
        dx = dx.astype(BF16)
        out_ref[...] = dx
        dxall_ref[rr, :] = dx


def turn_weights_kernel(win_ref, wout_ref, wint_ref, woutt_ref):
    wint_ref[...] = win_ref[...].T
    woutt_ref[...] = wout_ref[...].T


def turn_weights(win, wout):
    shapes = [jax.ShapeDtypeStruct(w.shape[::-1], BF16) for w in (win, wout)]
    return pl.pallas_call(
        turn_weights_kernel,
        out_shape=tuple(shapes),
        in_specs=whole(2),
        out_specs=tuple(whole(2)),
        compiler_params=pltpu.CompilerParams(vmem_limit_bytes=4 * MIB),
        name="turn_weights",
    )(win, wout)


def step(sc, packed, got, win, wout, saved, dpre, gall, dxall):
    q, k, v, gate, n2, att, ds, xn, r1, r2 = saved
    width = q.shape[1]
    return pl.pallas_call(
        step_kernel,
        out_shape=(
            jax.ShapeDtypeStruct((ROWS, width), BF16),
            jax.ShapeDtypeStruct(dpre.shape, BF16),
            jax.ShapeDtypeStruct(gall.shape, BF16),
            jax.ShapeDtypeStruct(dxall.shape, BF16),
        ),
        in_specs=[pl.BlockSpec(memory_space=pltpu.SMEM)] + whole(17),
        out_specs=tuple(whole(4)),
        input_output_aliases={15: 1, 16: 2, 17: 3},
        scratch_shapes=[pltpu.VMEM((ROWS, width), BF16)] * 2,
        compiler_params=pltpu.CompilerParams(vmem_limit_bytes=8 * MIB),
        name="step",
    )(sc, packed, got, win, wout, q, k, v, gate, n2, att, ds, xn, r1, r2, dpre, gall, dxall)


def weights_kernel(xnt_ref, yut_ref, dpre_ref, gall_ref, out_ref, buf, sem):
    width = gall_ref.shape[1]
    block = 1024
    first = 4 * width // block
    count = 5 * width // block

    def send(i, slot):
        there = pl.ds(pl.multiple_of(i * block, block), block)
        return pltpu.make_async_copy(buf.at[slot], out_ref.at[:, there], sem.at[slot])

    def run(i, carry):
        slot = lax.rem(i, 2)

        @pl.when(i >= 2)
        def _():
            send(i - 2, slot).wait()

        @pl.when(i < first)
        def _():
            cols = pl.ds(pl.multiple_of(i * block, block), block)
            buf[slot] = dot_nn(xnt_ref[...], dpre_ref[:, cols]).astype(BF16)

        @pl.when(i >= first)
        def _():
            cols = pl.ds(pl.multiple_of((i - first) * block, block), block)
            buf[slot] = dot_nn(yut_ref[...], gall_ref[:, cols]).astype(BF16)

        send(i, slot).start()
        return carry

    lax.fori_loop(0, count, run, 0)
    send(count - 2, lax.rem(count - 2, 2)).wait()
    send(count - 1, lax.rem(count - 1, 2)).wait()


def widen_kernel(sum_ref, win_ref, wout_ref):
    split = win_ref.shape[1]
    win_ref[...] = sum_ref[:, :split].astype(F32)
    wout_ref[...] = sum_ref[:, split:].astype(F32)


def body(saved_inputs, cotangent, pack_lists, segment_ids, w_in, w_out):
    dp_count = lax.axis_size("dp")
    section_count = lax.axis_size("section")
    section_index = lax.axis_index("section")
    tok_rows, width = cotangent.shape
    micro_count, mb_rows = segment_ids.shape
    share = tok_rows // dp_count
    hops = section_count - 1
    picked = cotangent[pack_lists[0]]
    tiled = jnp.tile(segment_ids, (1, GROUP))
    pos = jnp.arange(mb_rows)
    allowed = (segment_ids[:, :, None] == tiled[:, None, :]) & (
        (jnp.arange(WIDE) % mb_rows)[None, None, :] <= pos[None, :, None]
    )
    mask = allowed.astype(F32).reshape(tok_rows, WIDE)
    lag = lambda h: SKEW * h
    chunks = tok_rows // ROWS
    steps = chunks + lag(hops)
    slots = jnp.arange(steps, dtype=jnp.int32) - lag(hops - section_index)
    valid = ((slots >= 0) & (slots < chunks)).astype(jnp.int32)
    first = section_index == hops
    source = jnp.where(first, 0, 1).astype(jnp.int32)
    table = jnp.stack(
        [
            jnp.clip(slots, 0, chunks - 1),
            valid,
            jnp.broadcast_to(source, slots.shape),
        ],
        axis=1,
    )
    scalars = [table[t] for t in range(steps)]
    picked, mask, scalars, saved_inputs, w_in, w_out = lax.optimization_barrier(
        (picked, mask, scalars, saved_inputs, w_in, w_out)
    )
    packed = lax.all_to_all(
        picked.reshape(dp_count, share, width), "dp", split_axis=0, concat_axis=0, tiled=True
    ).reshape(tok_rows, width)
    made = forward(saved_inputs[0], mask, w_in[0])
    packed, made, w_in, w_out = lax.optimization_barrier((packed, made, w_in, w_out))
    win, wout = turn_weights(w_in[0], w_out[0])
    q, k, v, gate, n2, att, ds, dpre, xn, r1, r2 = made
    xnt, yut = turn(xn, n2, gate)
    saved = (q, k, v, gate, n2, att, ds, xn, r1, r2)

    down = [(s, s - 1) for s in range(1, section_count)]

    zero = jnp.zeros((ROWS, width), BF16)
    moving = {}
    keep = lambda a: pltpu.with_memory_space_constraint(a, VMEM)
    dpre = keep(dpre)
    gall = keep(jnp.zeros((tok_rows, width), BF16))
    dxall = keep(jnp.zeros((tok_rows, width), BF16))
    for t in range(steps):
        got = moving.pop(t - SKEW, zero)
        dx, dpre, gall, dxall = step(scalars[t], packed, got, win, wout, saved, dpre, gall, dxall)
        if t + SKEW < steps:
            moving[t] = lax.ppermute(dx, "section", down)

    store = pl.pallas_call(
        weights_kernel,
        out_shape=jax.ShapeDtypeStruct((width, 5 * width), BF16),
        in_specs=whole(4),
        out_specs=pl.BlockSpec(memory_space=pl.ANY),
        scratch_shapes=[pltpu.VMEM((2, width, 1024), BF16), pltpu.SemaphoreType.DMA((2,))],
        compiler_params=pltpu.CompilerParams(vmem_limit_bytes=34 * MIB),
        name="weights",
    )(xnt, yut, dpre, gall)
    summed = lax.psum_scatter(store, "dp", scatter_dimension=0, tiled=True)
    rows = summed.shape[0]
    grad_in, grad_out = pl.pallas_call(
        widen_kernel,
        out_shape=(
            jax.ShapeDtypeStruct((rows, 4 * width), F32),
            jax.ShapeDtypeStruct((rows, width), F32),
        ),
        in_specs=whole(1),
        out_specs=tuple(whole(2)),
        name="widen",
    )(summed)
    return (dxall[None], grad_in[None], grad_out[None])


def solution(mesh):
    return jax.shard_map(
        body,
        mesh=mesh,
        in_specs=(
            P("section", "dp", None),
            P("dp", None),
            P("dp", None),
            P("dp", None),
            P("section", None, None),
            P("section", None, None),
        ),
        out_specs=(P("section", "dp", None), P("section", "dp", None), P("section", "dp", None)),
        check_vma=False,
    )
```

```python
import jax
import jax.numpy as jnp
from jax import lax
from jax.experimental import pallas as pl
from jax.experimental.pallas import tpu as pltpu
from jax.sharding import PartitionSpec as P

H = 16
HEAD = 64
MB = 64
WIDE = 256
GROUP = WIDE // HEAD
EPS = 1e-05
SKEW = 2
ROWS = 2 * MB
MIB = 1 << 20
VMEM = pltpu.VMEM
F32 = jnp.float32
BF16 = jnp.bfloat16


def whole(count):
    return [pl.BlockSpec(memory_space=VMEM)] * count


def dot_nn(left, right):
    return lax.dot_general(left, right, (((1,), (0,)), ((), ())), preferred_element_type=F32)


def dot_nt(left, right):
    return lax.dot_general(left, right, (((1,), (1,)), ((), ())), preferred_element_type=F32)


def dot_tn(left, right):
    return lax.dot_general(left, right, (((0,), (0,)), ((), ())), preferred_element_type=F32)


def head_masks():
    lane = lax.broadcasted_iota(jnp.int32, (MB, WIDE), 1)
    return [((lane >= h * HEAD) & (lane < (h + 1) * HEAD)) for h in range(GROUP)]


def spread(block, masks):
    wide = block.astype(F32)
    return jnp.concatenate([jnp.where(m, wide, 0.0).astype(BF16) for m in masks], axis=0)


def gather_heads(full, masks):
    total = jnp.where(masks[0], full[:MB], 0.0)
    for h in range(1, GROUP):
        total = jnp.where(masks[h], full[h * MB : (h + 1) * MB], total)
    return total


def mean_rows(values):
    return jnp.sum(values, axis=-1, keepdims=True) * (1.0 / values.shape[-1])


def forward_kernel(
    x_ref, mask_ref, win_ref,
    q_ref, k_ref, v_ref, gate_ref, n2_ref, att_ref, ds_ref, dsil_ref, xn_ref, r1_ref, r2_ref, mixed,
):
    rows, width = x_ref.shape
    masks = head_masks()
    x = x_ref[...].astype(F32)
    centered = x - mean_rows(x)
    r1 = lax.rsqrt(mean_rows(centered * centered) + EPS)
    xn_ref[...] = (centered * r1).astype(BF16)
    r1_ref[...] = jnp.broadcast_to(r1, r1_ref.shape)
    outs = (gate_ref, v_ref, q_ref, k_ref)
    for cb in range(width // WIDE):
        cols = slice(cb * WIDE, (cb + 1) * WIDE)
        for part in range(4):
            wide = slice(part * width + cb * WIDE, part * width + (cb + 1) * WIDE)
            pre = dot_nn(xn_ref[...], win_ref[:, wide])
            sig = jax.nn.sigmoid(pre)
            act = pre * sig
            outs[part][:, cols] = act.astype(BF16)
            dsil_ref[:, wide] = (sig + act * (1.0 - sig)).astype(BF16)
        for m in range(rows // MB):
            rr = slice(m * MB, (m + 1) * MB)
            k4 = spread(k_ref[rr, cols], masks)
            v4 = spread(v_ref[rr, cols], masks)
            s = dot_nt(q_ref[rr, cols], k4) * (1.0 / 8.0)
            mask = mask_ref[rr, :]
            sg = jax.nn.sigmoid(s)
            sil = s * sg
            att = (sil * mask * (1.0 / MB)).astype(BF16)
            att_ref[rr, cols] = att
            ds_ref[rr, cols] = ((sg + sil * (1.0 - sg)) * mask * (1.0 / (8 * MB))).astype(BF16)
            mixed[rr, cols] = dot_nn(att, v4)
    mx = mixed[...]
    cm = mx - mean_rows(mx)
    r2 = lax.rsqrt(mean_rows(cm * cm) + EPS)
    r2_ref[...] = jnp.broadcast_to(r2, r2_ref.shape)
    n2_ref[...] = (cm * r2).astype(BF16)


def transpose_kernel(xn_ref, n2_ref, gate_ref, xnt_ref, yut_ref):
    xnt_ref[...] = xn_ref[...].T
    yu = n2_ref[...].astype(F32) * gate_ref[...].astype(F32)
    yut_ref[...] = yu.astype(BF16).T


def forward(x, mask, win):
    rows, width = x.shape
    block = 4 * MB
    small = jax.ShapeDtypeStruct((rows, width), BF16)
    big = jax.ShapeDtypeStruct((rows, 4 * width), BF16)
    stat = jax.ShapeDtypeStruct((rows, 128), F32)
    shapes = (small,) * 7 + (big, small, stat, stat)
    lines = lambda a: pl.BlockSpec((block, a.shape[1]), lambda i: (i, 0))
    return pl.pallas_call(
        forward_kernel,
        out_shape=shapes,
        grid=(rows // block,),
        in_specs=[
            lines(x),
            lines(mask),
            pl.BlockSpec(win.shape, lambda i: (0, 0), pipeline_mode=pl.Buffered(1)),
        ],
        out_specs=tuple(lines(a) for a in shapes),
        scratch_shapes=[pltpu.VMEM((block, width), F32)],
        compiler_params=pltpu.CompilerParams(vmem_limit_bytes=58 * MIB),
        name="forward",
    )(x, mask, win)


def turn(xn, n2, gate):
    turned = jax.ShapeDtypeStruct(xn.shape[::-1], BF16)
    return pl.pallas_call(
        transpose_kernel,
        out_shape=(turned, turned),
        in_specs=whole(3),
        out_specs=tuple(whole(2)),
        compiler_params=pltpu.CompilerParams(vmem_limit_bytes=8 * MIB),
        name="turn",
    )(xn, n2, gate)


def step_kernel(
    sc_ref, packed_ref, got_ref, win_ref, wout_ref, q_ref, k_ref, v_ref, gate_ref, n2_ref, att_ref,
    ds_ref, xn_ref, r1_ref, r2_ref, dpre_in, gall_in, dxall_in,
    out_ref, dpre_ref, gall_ref, dxall_ref, gbuf,
):
    slot, valid, source = sc_ref[0], sc_ref[1], sc_ref[2]
    width = out_ref.shape[1]

    @pl.when(valid == 1)
    def _():
        rr = pl.ds(pl.multiple_of(slot * ROWS, ROWS), ROWS)

        @pl.when(source == 0)
        def _():
            gbuf[...] = packed_ref[rr, :]

        @pl.when(source == 1)
        def _():
            gbuf[...] = got_ref[...]

        masks = head_masks()
        g = gbuf[...]
        gall_ref[rr, :] = g
        d_yu = dot_nn(g, wout_ref[...]).astype(BF16).astype(F32)
        n2 = n2_ref[rr, :].astype(F32)
        gate = gate_ref[rr, :].astype(F32)
        d_gate = d_yu * n2
        d_n2 = d_yu * gate
        r2 = r2_ref[rr, :][:, :1]
        d_mixed = (r2 * (d_n2 - mean_rows(d_n2) - n2 * mean_rows(d_n2 * n2))).astype(BF16)
        dpre_ref[rr, :width] = (d_gate * dpre_in[rr, :width].astype(F32)).astype(BF16)
        for c in range(width // WIDE):
            lo = c * WIDE
            cols = slice(lo, lo + WIDE)
            for m in range(ROWS // MB):
                mm = pl.ds(pl.multiple_of(slot * ROWS + m * MB, MB), MB)
                do4 = d_mixed[m * MB : (m + 1) * MB, cols]
                q4 = q_ref[mm, cols]
                k4 = spread(k_ref[mm, cols], masks)
                v4 = spread(v_ref[mm, cols], masks)
                att = att_ref[mm, cols]
                d_att = dot_nt(do4, v4)
                d_s = (d_att * ds_ref[mm, cols].astype(F32)).astype(BF16)
                d_q = dot_nn(d_s, k4)
                d_k = gather_heads(dot_tn(d_s, q4), masks)
                d_v = gather_heads(dot_tn(att, do4), masks)
                for part, val in ((1, d_v), (2, d_q), (3, d_k)):
                    at = slice(part * width + lo, part * width + lo + WIDE)
                    dpre_ref[mm, at] = (val * dpre_in[mm, at].astype(F32)).astype(BF16)
        d_xn = dot_nn(dpre_ref[rr, :], win_ref[...])
        xn = xn_ref[rr, :].astype(F32)
        r1 = r1_ref[rr, :][:, :1]
        dx = g.astype(F32) + r1 * (d_xn - mean_rows(d_xn) - xn * mean_rows(d_xn * xn))
        dx = dx.astype(BF16)
        out_ref[...] = dx
        dxall_ref[rr, :] = dx


def turn_weights_kernel(win_ref, wout_ref, wint_ref, woutt_ref):
    wint_ref[...] = win_ref[...].T
    woutt_ref[...] = wout_ref[...].T


def turn_weights(win, wout):
    shapes = [jax.ShapeDtypeStruct(w.shape[::-1], BF16) for w in (win, wout)]
    return pl.pallas_call(
        turn_weights_kernel,
        out_shape=tuple(shapes),
        in_specs=whole(2),
        out_specs=tuple(whole(2)),
        compiler_params=pltpu.CompilerParams(vmem_limit_bytes=4 * MIB),
        name="turn_weights",
    )(win, wout)


def step(sc, packed, got, win, wout, saved, dpre, gall, dxall):
    q, k, v, gate, n2, att, ds, xn, r1, r2 = saved
    width = q.shape[1]
    return pl.pallas_call(
        step_kernel,
        out_shape=(
            jax.ShapeDtypeStruct((ROWS, width), BF16),
            jax.ShapeDtypeStruct(dpre.shape, BF16),
            jax.ShapeDtypeStruct(gall.shape, BF16),
            jax.ShapeDtypeStruct(dxall.shape, BF16),
        ),
        in_specs=[pl.BlockSpec(memory_space=pltpu.SMEM)] + whole(17),
        out_specs=tuple(whole(4)),
        input_output_aliases={15: 1, 16: 2, 17: 3},
        scratch_shapes=[pltpu.VMEM((ROWS, width), BF16)],
        compiler_params=pltpu.CompilerParams(vmem_limit_bytes=8 * MIB),
        name="step",
    )(sc, packed, got, win, wout, q, k, v, gate, n2, att, ds, xn, r1, r2, dpre, gall, dxall)


def weights_kernel(xnt_ref, yut_ref, dpre_ref, gall_ref, out_ref, buf, sem):
    width = gall_ref.shape[1]
    block = 1024
    first = 4 * width // block
    count = 5 * width // block

    def send(i, slot):
        there = pl.ds(pl.multiple_of(i * block, block), block)
        return pltpu.make_async_copy(buf.at[slot], out_ref.at[:, there], sem.at[slot])

    def run(i, carry):
        slot = lax.rem(i, 2)

        @pl.when(i >= 2)
        def _():
            send(i - 2, slot).wait()

        @pl.when(i < first)
        def _():
            cols = pl.ds(pl.multiple_of(i * block, block), block)
            buf[slot] = dot_nn(xnt_ref[...], dpre_ref[:, cols]).astype(BF16)

        @pl.when(i >= first)
        def _():
            cols = pl.ds(pl.multiple_of((i - first) * block, block), block)
            buf[slot] = dot_nn(yut_ref[...], gall_ref[:, cols]).astype(BF16)

        send(i, slot).start()
        return carry

    lax.fori_loop(0, count, run, 0)
    send(count - 2, lax.rem(count - 2, 2)).wait()
    send(count - 1, lax.rem(count - 1, 2)).wait()


def widen_kernel(sum_ref, win_ref, wout_ref):
    split = win_ref.shape[1]
    win_ref[...] = sum_ref[:, :split].astype(F32)
    wout_ref[...] = sum_ref[:, split:].astype(F32)


def body(saved_inputs, cotangent, pack_lists, segment_ids, w_in, w_out):
    dp_count = lax.axis_size("dp")
    section_count = lax.axis_size("section")
    section_index = lax.axis_index("section")
    tok_rows, width = cotangent.shape
    micro_count, mb_rows = segment_ids.shape
    share = tok_rows // dp_count
    hops = section_count - 1
    picked = cotangent[pack_lists[0]]
    tiled = jnp.tile(segment_ids, (1, GROUP))
    pos = jnp.arange(mb_rows)
    allowed = (segment_ids[:, :, None] == tiled[:, None, :]) & (
        (jnp.arange(WIDE) % mb_rows)[None, None, :] <= pos[None, :, None]
    )
    mask = allowed.astype(F32).reshape(tok_rows, WIDE)
    lag = lambda h: SKEW * h
    chunks = tok_rows // ROWS
    steps = chunks + lag(hops)
    slots = jnp.arange(steps, dtype=jnp.int32) - lag(hops - section_index)
    valid = ((slots >= 0) & (slots < chunks)).astype(jnp.int32)
    first = section_index == hops
    source = jnp.where(first, 0, 1).astype(jnp.int32)
    table = jnp.stack(
        [
            jnp.clip(slots, 0, chunks - 1),
            valid,
            jnp.broadcast_to(source, slots.shape),
        ],
        axis=1,
    )
    scalars = [table[t] for t in range(steps)]
    picked, mask, scalars, saved_inputs, w_in, w_out = lax.optimization_barrier(
        (picked, mask, scalars, saved_inputs, w_in, w_out)
    )
    packed = lax.all_to_all(
        picked.reshape(dp_count, share, width), "dp", split_axis=0, concat_axis=0, tiled=True
    ).reshape(tok_rows, width)
    made = forward(saved_inputs[0], mask, w_in[0])
    packed, made, w_in, w_out = lax.optimization_barrier((packed, made, w_in, w_out))
    win, wout = turn_weights(w_in[0], w_out[0])
    q, k, v, gate, n2, att, ds, dpre, xn, r1, r2 = made
    xnt, yut = turn(xn, n2, gate)
    saved = (q, k, v, gate, n2, att, ds, xn, r1, r2)

    down = [(s, s - 1) for s in range(1, section_count)]

    zero = jnp.zeros((ROWS, width), BF16)
    moving = {}
    keep = lambda a: pltpu.with_memory_space_constraint(a, VMEM)
    dpre = keep(dpre)
    gall = keep(jnp.zeros((tok_rows, width), BF16))
    dxall = keep(jnp.zeros((tok_rows, width), BF16))
    for t in range(steps):
        got = moving.pop(t - SKEW, zero)
        dx, dpre, gall, dxall = step(scalars[t], packed, got, win, wout, saved, dpre, gall, dxall)
        if t + SKEW < steps:
            moving[t] = lax.ppermute(dx, "section", down)

    store = pl.pallas_call(
        weights_kernel,
        out_shape=jax.ShapeDtypeStruct((width, 5 * width), BF16),
        in_specs=whole(4),
        out_specs=pl.BlockSpec(memory_space=pl.ANY),
        scratch_shapes=[pltpu.VMEM((2, width, 1024), BF16), pltpu.SemaphoreType.DMA((2,))],
        compiler_params=pltpu.CompilerParams(vmem_limit_bytes=34 * MIB),
        name="weights",
    )(xnt, yut, dpre, gall)
    summed = lax.psum_scatter(store, "dp", scatter_dimension=0, tiled=True)
    rows = summed.shape[0]
    grad_in, grad_out = pl.pallas_call(
        widen_kernel,
        out_shape=(
            jax.ShapeDtypeStruct((rows, 4 * width), F32),
            jax.ShapeDtypeStruct((rows, width), F32),
        ),
        in_specs=whole(1),
        out_specs=tuple(whole(2)),
        name="widen",
    )(summed)
    return (dxall[None], grad_in[None], grad_out[None])


def solution(mesh):
    return jax.shard_map(
        body,
        mesh=mesh,
        in_specs=(
            P("section", "dp", None),
            P("dp", None),
            P("dp", None),
            P("dp", None),
            P("section", None, None),
            P("section", None, None),
        ),
        out_specs=(P("section", "dp", None), P("section", "dp", None), P("section", "dp", None)),
        check_vma=False,
    )
```
